32 devices in a mesh: seq: 4 (over z), pipe: 4 (over y, core), exp: 2 (over x).
Axes of the slice: x: 2, y: 2, z: 4, core: 2. Of those that a mesh axis runs over, the one named last changes fastest.
Arguments:
- queries: bfloat16 [4, 32, 512, 128], P('pipe', 'exp', 'seq'), may hold values from -0.75 to 0.75
- keys: bfloat16 [4, 32, 512, 128], P('pipe', 'exp', 'seq'), may hold values from -0.75 to 0.75
- values: bfloat16 [4, 32, 512, 128], P('pipe', 'exp', 'seq'), may hold values from -0.75 to 0.75
- grad_out: bfloat16 [4, 32, 512, 128], P('pipe', 'exp', 'seq'), may hold values from -0.75 to 0.75
- log_decay: float32 [4, 32, 512], P('pipe', 'exp', 'seq'), may hold values from -2 to 0
Outputs:
- next_input: bfloat16 [4, 512, 4096], P('pipe', ('seq', 'exp'))
- grad_queries: bfloat16 [4, 32, 512, 128], P('pipe', 'exp', 'seq')
- grad_keys: bfloat16 [4, 32, 512, 128], P('pipe', 'exp', 'seq')
- grad_values: bfloat16 [4, 32, 512, 128], P('pipe', 'exp', 'seq')
The draws below stay inside these ranges and needn't reach their ends.
All inputs are finite; a program needn't handle non-finite values.
Results may differ from the reference program's by a relative error of at most 0.0063.
Values may be sent and summed in bfloat16 or wider, within the bound.
A program may use at most 128 MiB of HBM per device.

```python
import math
import jax
import jax.numpy as jnp
from jax import lax

HEAD_COUNT = 32
HEAD_DIM = 128
TOK_DEV = 128
SEQUENCE_LENGTH = 512
RELAY_SECTIONS = 4


def draw_log_decay(key, part):
    fast_share = 0.5
    head_picks = jax.random.uniform(jax.random.fold_in(key, 1), (RELAY_SECTIONS, HEAD_COUNT, 1))
    fast_heads = head_picks < fast_share
    slow_rate = 0.15 * math.log(10.0) / SEQUENCE_LENGTH
    fast_rate = 6.0 / TOK_DEV
    baseline_rate = jnp.where(fast_heads, fast_rate, slow_rate)
    jitter_amount = jnp.exp(jax.random.uniform(jax.random.fold_in(key, 2), (RELAY_SECTIONS, HEAD_COUNT, SEQUENCE_LENGTH), minval=-math.log(2.0), maxval=math.log(2.0)))
    block_count = SEQUENCE_LENGTH // TOK_DEV
    block_multiplier = jnp.exp(jax.random.uniform(jax.random.fold_in(key, 3), (RELAY_SECTIONS, HEAD_COUNT, block_count, 1), minval=-math.log(2.0), maxval=math.log(2.0)))
    block_multiplier = jnp.broadcast_to(block_multiplier, (RELAY_SECTIONS, HEAD_COUNT, block_count, TOK_DEV)).reshape(RELAY_SECTIONS, HEAD_COUNT, SEQUENCE_LENGTH)
    spike_positions = jax.random.randint(jax.random.fold_in(key, 4), (RELAY_SECTIONS, 2), 0, SEQUENCE_LENGTH)
    position_index = jnp.arange(SEQUENCE_LENGTH)
    spike_events = jnp.any(position_index[None, :, None] == spike_positions[:, None, :], axis=2)
    spike_decreases = jax.random.uniform(jax.random.fold_in(key, 5), (RELAY_SECTIONS, HEAD_COUNT, SEQUENCE_LENGTH), minval=math.log(0.5), maxval=math.log(0.8))
    return -baseline_rate * jitter_amount * block_multiplier + jnp.where(spike_events[:, None, :], spike_decreases, 0.0)


def shard_levels(stream_key, dims, cuts, least, high):
    def one(position, shards_of):
        draws = jax.random.uniform(jax.random.fold_in(jax.random.fold_in(stream_key, 6), position), (shards_of,), jnp.float32, least / len(cuts), high / len(cuts))
        return jnp.repeat(jnp.exp(draws), dims[position] // shards_of).reshape((-1,) + (1,) * (len(dims) - position - 1))

    gain = one(*cuts[0])
    for cut in cuts[1:]:
        gain = gain * one(*cut)
    return gain


def centred(own_key, shape, width, reach, pieces=(), dtype=jnp.bfloat16):
    entries = jax.random.normal(own_key, shape, jnp.float32) * width
    if len(pieces) > 0:
        entries = shard_levels(own_key, shape, pieces, -0.22, 0.18) * entries
    return jnp.clip(entries, min=-reach, max=reach).astype(dtype)


def setup_inputs(seed: int = 0) -> dict:
    streams_of = jax.random.split(jax.random.key(seed), 6)
    queries = centred(streams_of[0], (RELAY_SECTIONS, HEAD_COUNT, SEQUENCE_LENGTH, HEAD_DIM), 0.125, 0.75, ((0, 4), (1, 2), (2, 4)))
    keys = centred(streams_of[1], (RELAY_SECTIONS, HEAD_COUNT, SEQUENCE_LENGTH, HEAD_DIM), 0.125, 0.75, ((0, 4), (1, 2), (2, 4)))
    values = centred(streams_of[2], (RELAY_SECTIONS, HEAD_COUNT, SEQUENCE_LENGTH, HEAD_DIM), 0.125, 0.75, ((0, 4), (1, 2), (2, 4)))
    grad_out = centred(streams_of[3], (RELAY_SECTIONS, HEAD_COUNT, SEQUENCE_LENGTH, HEAD_DIM), 0.125, 0.75, ((0, 4), (1, 2), (2, 4)))
    log_decay = draw_log_decay(jax.random.fold_in(streams_of[5], 71), 0)
    return dict(queries=queries, keys=keys, values=values, grad_out=grad_out, log_decay=log_decay)


def rounded(array):
    return lax.optimization_barrier(array.astype(jnp.bfloat16)).astype(jnp.float32)


def product(form, left, right):
    return jnp.einsum(form, left.astype(jnp.float32), right.astype(jnp.float32), precision=lax.Precision.HIGHEST)


def block_terms(block_items):
    query_heads, key_heads, value_heads, grad_heads, log_rate = block_items
    row_count = query_heads.shape[1]
    cumulative = jnp.cumsum(log_rate, axis=1)
    block_total = cumulative[:, -1]
    position_index = jnp.arange(row_count)
    causal = position_index[:, None] >= position_index[None, :]
    spread = cumulative[:, :, None] - cumulative[:, None, :]
    weight = jnp.exp(jnp.where(causal[None], spread, -1e30))
    weighted = rounded(product("hid,hjd->hij", query_heads, key_heads) * weight)
    weighted_grad = rounded(product("hie,hje->hij", grad_heads, value_heads) * weight)
    decay_in = jnp.exp(cumulative)[:, :, None]
    decay_out = jnp.exp(block_total[:, None] - cumulative)[:, :, None]
    query_decayed = rounded(query_heads.astype(jnp.float32) * decay_in)
    key_decayed = rounded(key_heads.astype(jnp.float32) * decay_out)
    block_state = product("hjd,hje->hde", key_decayed, value_heads)
    grad_state = product("hid,hie->hde", query_decayed, grad_heads)
    block_gain = jnp.exp(block_total)
    return weighted, weighted_grad, query_decayed, key_decayed, block_state, grad_state, block_gain, cumulative


def finish_block(block_items):
    (weighted, weighted_grad, query_decayed, key_decayed, query_heads, key_heads,
     value_heads, grad_heads, prefix, suffix, cumulative) = block_items
    block_total = cumulative[:, -1]
    decay_in = jnp.exp(cumulative)[:, :, None]
    decay_out = jnp.exp(block_total[:, None] - cumulative)[:, :, None]
    prefix_low = rounded(prefix)
    suffix_low = rounded(suffix)
    attention_out = product("hij,hje->hie", weighted, value_heads) + product("hid,hde->hie", query_decayed, prefix_low)
    grad_query = product("hij,hjd->hid", weighted_grad, key_heads) + product("hie,hde->hid", grad_heads, prefix_low) * decay_in
    grad_key = product("hij,hid->hjd", weighted_grad, query_heads) + product("hje,hde->hjd", value_heads, suffix_low) * decay_out
    grad_value = product("hij,hie->hje", weighted, grad_heads) + product("hjd,hde->hje", key_decayed, suffix_low)
    return (attention_out.astype(jnp.bfloat16), grad_query.astype(jnp.bfloat16),
            grad_key.astype(jnp.bfloat16), grad_value.astype(jnp.bfloat16))


def forward_step(state, item):
    block_gain, block_state = item
    return block_gain[:, None, None] * state + block_state, state


def one_section(section_items):
    queries, keys, values, grad_out, log_decay = section_items
    block_count = SEQUENCE_LENGTH // TOK_DEV
    block_shape = (HEAD_COUNT, block_count, TOK_DEV, HEAD_DIM)
    query_heads = queries.reshape(block_shape).transpose(1, 0, 2, 3)
    key_heads = keys.reshape(block_shape).transpose(1, 0, 2, 3)
    value_heads = values.reshape(block_shape).transpose(1, 0, 2, 3)
    grad_heads = grad_out.reshape(block_shape).transpose(1, 0, 2, 3)
    log_rate = log_decay.reshape(HEAD_COUNT, block_count, TOK_DEV).transpose(1, 0, 2)
    terms = lax.map(block_terms, (query_heads, key_heads, value_heads, grad_heads, log_rate))
    weighted, weighted_grad, query_decayed, key_decayed, block_state, grad_state, block_gain, cumulative = terms
    start = jnp.zeros((HEAD_COUNT, HEAD_DIM, HEAD_DIM), jnp.float32)
    _, prefix = lax.scan(forward_step, start, (block_gain, block_state))
    _, suffix = lax.scan(forward_step, start, (block_gain, grad_state), reverse=True)
    results = lax.map(finish_block, (weighted, weighted_grad, query_decayed, key_decayed, query_heads,
                                     key_heads, value_heads, grad_heads, prefix, suffix, cumulative))
    attention_out = results[0].transpose(0, 2, 1, 3).reshape(SEQUENCE_LENGTH, HEAD_COUNT * HEAD_DIM)
    grads = tuple(part.transpose(1, 0, 2, 3).reshape(HEAD_COUNT, SEQUENCE_LENGTH, HEAD_DIM) for part in results[1:])
    return (attention_out,) + grads


def reference(queries, keys, values, grad_out, log_decay):
    attention_out, grad_queries, grad_keys, grad_values = lax.map(one_section, (queries, keys, values, grad_out, log_decay))
    next_input = jnp.concatenate([jnp.zeros_like(attention_out[:1]), attention_out[:-1]], axis=0)
    return next_input, grad_queries, grad_keys, grad_values
```

```python
import functools
import math

import jax
import jax.numpy as jnp
from jax import lax
from jax.experimental import pallas as pl
from jax.experimental.pallas import tpu as pltpu
from jax.sharding import PartitionSpec as P

MESH = pl.DeviceIdType.MESH
LAG = 5
GROUP = 4
VMEM_LIMIT = 61 * 2**20


def dot(left, right, dims):
    return lax.dot_general(left, right, ((dims[:1], dims[1:]), ((), ())), preferred_element_type=jnp.float32)


def kernel(
    sizes, group, q_in, k_in, v_in, g_in, decay_in_ref, next_ref, gq_ref, gk_ref, gv_ref,
    q_ref, k_ref, v_ref, g_ref, decay_ref, cum, state, grad_state, weighted, weighted_grad, q_dec, k_dec, decay_in, decay_out, columns,
    prefix, suffix, up, down, attn,
    in_sem, decay_sem, prefix_sem, suffix_sem, up_sem, down_sem, attn_sem, next_sem, ready,
):
    seq_count, pipe_count, exp_count = sizes
    seq, pipe, exp = lax.axis_index("seq"), lax.axis_index("pipe"), lax.axis_index("exp")
    heads, rows, dim = q_ref.shape
    groups = heads // group
    part_rows = rows // exp_count
    has_below, has_above = seq > 0, seq < seq_count - 1
    receives, sends = pipe > 0, pipe < pipe_count - 1
    even = pipe % 2 == 0

    decay_copy = pltpu.make_async_copy(decay_in_ref, decay_ref, decay_sem)
    decay_copy.start()

    def in_copies(first):
        at = pl.ds(first * group, group)
        pairs = ((k_in, k_ref), (q_in, q_ref), (v_in, v_ref), (g_in, g_ref))
        return [pltpu.make_async_copy(src.at[at], dst.at[at], in_sem.at[i, first]) for i, (src, dst) in enumerate(pairs)]

    @pl.loop(0, groups)
    def _(t):
        for copy in in_copies(t):
            copy.start()

    barrier = pltpu.get_barrier_semaphore()

    def greet(condition, device):
        @pl.when(condition)
        def _():
            pl.semaphore_signal(barrier, inc=1, device_id=device, device_id_type=MESH)

    greet(has_below, {"seq": seq - 1})
    greet(has_above, {"seq": seq + 1})

    def enter_kernel():
        beside = has_below.astype(jnp.int32) + has_above.astype(jnp.int32)
        relayed = receives.astype(jnp.int32) + sends.astype(jnp.int32)

        @pl.when(even)
        def _():
            pl.semaphore_wait(barrier, beside)
            for other in range(exp_count):
                greet(receives, {"pipe": pipe - 1, "exp": other})
                greet(sends, {"pipe": pipe + 1, "exp": other})

        @pl.when(jnp.logical_not(even))
        def _():
            pl.semaphore_wait(barrier, beside + exp_count * relayed)
            for other in range(exp_count):
                pl.semaphore_signal(ready, inc=1, device_id={"pipe": pipe - 1, "exp": other}, device_id_type=MESH)

    @pl.when(jnp.logical_not(has_below))
    def _():
        prefix[...] = jnp.zeros_like(prefix)

    @pl.when(jnp.logical_not(has_above))
    def _():
        suffix[...] = jnp.zeros_like(suffix)

    @pl.when(jnp.logical_not(receives))
    def _():
        next_ref[...] = jnp.zeros_like(next_ref)

    decay_copy.wait()
    total = decay_ref[...]
    lane = lax.broadcasted_iota(jnp.int32, total.shape, 1)
    step = 1
    while step < rows:
        total = total + jnp.where(lane >= step, pltpu.roll(total, step, 1), 0.0)
        step *= 2
    cum[...] = total

    def up_copy(h):
        return pltpu.make_async_remote_copy(
            src_ref=up.at[h], dst_ref=prefix.at[h], send_sem=up_sem, recv_sem=prefix_sem.at[h],
            device_id={"seq": seq + 1}, device_id_type=MESH)

    def down_copy(h):
        return pltpu.make_async_remote_copy(
            src_ref=down.at[h], dst_ref=suffix.at[h], send_sem=down_sem, recv_sem=suffix_sem.at[h],
            device_id={"seq": seq - 1}, device_id_type=MESH)

    def attn_copy(head, other):
        place = pl.ds(pl.multiple_of((exp * heads + head) * dim, dim), dim)
        return pltpu.make_async_remote_copy(
            src_ref=attn.at[head, pl.ds(other * part_rows, part_rows)], dst_ref=next_ref.at[:, place],
            send_sem=attn_sem, recv_sem=next_sem,
            device_id={"pipe": pipe + 1, "exp": other}, device_id_type=MESH)

    def states(first):
        for copy in in_copies(first):
            copy.wait()
        for i in range(group):
            h = first * group + i
            down_rows = jnp.broadcast_to(cum[pl.ds(h, 1), :], (rows, rows)).T
            enter = jnp.exp(down_rows)
            leave = jnp.exp(down_rows[rows - 1:, :] - down_rows)
            qd = (q_ref[h].astype(jnp.float32) * enter[:, :dim]).astype(jnp.bfloat16)
            kd = (k_ref[h].astype(jnp.float32) * leave[:, :dim]).astype(jnp.bfloat16)
            own = dot(kd, v_ref[h], (0, 0))
            own_grad = dot(qd, g_ref[h], (0, 0))
            state[h], grad_state[h] = own, own_grad
            up[h], down[h] = own.astype(jnp.bfloat16), own_grad.astype(jnp.bfloat16)
            q_dec[h], k_dec[h] = qd, kd
            decay_in[h], decay_out[h], columns[h] = enter, leave, down_rows

    def send_states(first):
        @pl.when(jnp.logical_not(has_below))
        def _():
            for i in range(group):
                up_copy(first * group + i).start()

        @pl.when(jnp.logical_not(has_above))
        def _():
            for i in range(group):
                down_copy(first * group + i).start()

    def within(first):
        causal = lax.broadcasted_iota(jnp.int32, (rows, rows), 0) >= lax.broadcasted_iota(jnp.int32, (rows, rows), 1)
        for i in range(group):
            h = first * group + i
            weight = jnp.exp(jnp.where(causal, columns[h] - cum[pl.ds(h, 1), :], -1e30))
            weighted[h] = (dot(q_ref[h], k_ref[h], (1, 1)) * weight).astype(jnp.bfloat16)
            weighted_grad[h] = (dot(g_ref[h], v_ref[h], (1, 1)) * weight).astype(jnp.bfloat16)

    def forward(h):
        @pl.when(has_below)
        def _():
            up_copy(h).wait_recv()

            @pl.when(has_above)
            def _():
                gain = decay_in[h, rows - 1:, :]
                up[h] = (gain * prefix[h].astype(jnp.float32) + state[h]).astype(jnp.bfloat16)
                up_copy(h).start()

    def backward(h):
        @pl.when(has_above)
        def _():
            down_copy(h).wait_recv()

            @pl.when(has_below)
            def _():
                gain = decay_in[h, rows - 1:, :]
                down[h] = (gain * suffix[h].astype(jnp.float32) + grad_state[h]).astype(jnp.bfloat16)
                down_copy(h).start()

    def finish_forward(h):
        low = prefix[h]
        out = dot(weighted[h], v_ref[h], (1, 0)) + dot(q_dec[h], low, (1, 0))
        attn[h] = out.astype(jnp.bfloat16)
        gq = dot(weighted_grad[h], k_ref[h], (1, 0)) + dot(g_ref[h], low, (1, 1)) * decay_in[h]
        gq_ref[h] = gq.astype(jnp.bfloat16)

    def send_out(h):
        @pl.when(sends)
        def _():
            for other in range(exp_count):
                attn_copy(h, other).start()

    def finish_backward(h):
        low = suffix[h]
        gk = dot(weighted_grad[h], q_ref[h], (0, 0)) + dot(v_ref[h], low, (1, 1)) * decay_out[h]
        gk_ref[h] = gk.astype(jnp.bfloat16)
        gv = dot(weighted[h], g_ref[h], (0, 0)) + dot(k_dec[h], low, (1, 0))
        gv_ref[h] = gv.astype(jnp.bfloat16)

    states(0)
    enter_kernel()
    send_states(0)

    @pl.loop(1, groups)
    def _(t):
        states(t)
        send_states(t)

    @pl.loop(0, groups)
    def _(t):
        within(t)

    @pl.when(even & sends)
    def _():
        pl.semaphore_wait(ready, exp_count)

    @pl.loop(0, heads + LAG * (seq_count - 1))
    def _(t):
        ahead = t - LAG * seq
        behind = t - LAG * (seq_count - 1 - seq)
        moves_up = (ahead >= 0) & (ahead < heads)
        moves_down = (behind >= 0) & (behind < heads)

        @pl.when(moves_down)
        def _():
            backward(behind)

        @pl.when(moves_up)
        def _():
            forward(ahead)

        @pl.when(moves_up & moves_down)
        def _():
            finish_forward(ahead)
            finish_backward(behind)

        @pl.when(moves_up & jnp.logical_not(moves_down))
        def _():
            finish_forward(ahead)

        @pl.when(moves_down & jnp.logical_not(moves_up))
        def _():
            finish_backward(behind)

        @pl.when(moves_up)
        def _():
            send_out(ahead)

    @pl.when(has_above)
    def _():
        pltpu.make_async_copy(up, up, up_sem).wait()

    @pl.when(has_below)
    def _():
        pltpu.make_async_copy(down, down, down_sem).wait()

    @pl.when(sends)
    def _():
        pltpu.make_async_copy(attn, attn, attn_sem).wait()

    @pl.when(receives)
    def _():
        pltpu.make_async_copy(next_ref, next_ref, next_sem).wait()


def store(*refs):
    sem = refs[8]
    copies = [pltpu.make_async_copy(refs[i], refs[4 + i], sem.at[i]) for i in range(4)]
    for copy in copies:
        copy.start()
    for copy in copies:
        copy.wait()


def body(sizes, queries, keys, values, grad_out, log_decay):
    seq_count, pipe_count, exp_count = sizes
    _, heads, rows, dim = queries.shape
    group = math.gcd(GROUP, heads)
    low = jax.ShapeDtypeStruct((heads, rows, dim), jnp.bfloat16)
    vmem = pl.BlockSpec(memory_space=pltpu.VMEM)
    low_buf = pltpu.VMEM((heads, rows, dim), jnp.bfloat16)
    state_low = pltpu.VMEM((heads, dim, dim), jnp.bfloat16)
    state_wide = pltpu.VMEM((heads, dim, dim), jnp.float32)
    square_low = pltpu.VMEM((heads, rows, rows), jnp.bfloat16)
    square_wide = pltpu.VMEM((heads, rows, rows), jnp.float32)
    dma = pltpu.SemaphoreType.DMA
    any_place = pl.BlockSpec(memory_space=pl.ANY)
    next_rows = (rows // exp_count, exp_count * heads * dim)
    outs = pl.pallas_call(
        functools.partial(kernel, sizes, group),
        out_shape=(pltpu.VMEM(next_rows, jnp.bfloat16), low_buf, low_buf, low_buf),
        in_specs=[pl.BlockSpec(memory_space=pltpu.HBM)] * 5,
        out_specs=(vmem,) * 4,
        scratch_shapes=[
            low_buf, low_buf, low_buf, low_buf, pltpu.VMEM((heads, rows), jnp.float32),
            pltpu.VMEM((heads, rows), jnp.float32), state_wide, state_wide, square_low, square_low,
            low_buf, low_buf, square_wide, square_wide, square_wide,
            state_low, state_low, state_low, state_low, low_buf,
            dma((4, heads // group)), dma, dma((heads,)), dma((heads,)), dma, dma, dma, dma, pltpu.SemaphoreType.REGULAR,
        ],
        compiler_params=pltpu.CompilerParams(collective_id=0, has_side_effects=True, vmem_limit_bytes=VMEM_LIMIT),
    )(*(pltpu.with_memory_space_constraint(part[0], pltpu.HBM) for part in (queries, keys, values, grad_out, log_decay)))
    outs = pl.pallas_call(
        store,
        out_shape=(jax.ShapeDtypeStruct(next_rows, jnp.bfloat16), low, low, low),
        in_specs=[any_place] * 4,
        out_specs=(any_place,) * 4,
        scratch_shapes=[dma((4,))],
        compiler_params=pltpu.CompilerParams(vmem_limit_bytes=2**20),
    )(*outs)
    return tuple(out[None] for out in outs)


def solution(mesh):
    placed = P("pipe", "exp", "seq", None)
    sizes = tuple(mesh.shape[axis] for axis in ("seq", "pipe", "exp"))
    return jax.shard_map(
        functools.partial(body, sizes),
        mesh=mesh,
        in_specs=(placed, placed, placed, placed, P("pipe", "exp", "seq")),
        out_specs=(P("pipe", ("seq", "exp"), None), placed, placed, placed),
        check_vma=False,
    )
```

```python
import functools
import math

import jax
import jax.numpy as jnp
from jax import lax
from jax.experimental import pallas as pl
from jax.experimental.pallas import tpu as pltpu
from jax.sharding import PartitionSpec as P

MESH = pl.DeviceIdType.MESH
LAG = 5
GROUP = 4
HOLD = 3
VMEM_LIMIT = 61 * 2**20


def dot(left, right, dims):
    return lax.dot_general(left, right, ((dims[:1], dims[1:]), ((), ())), preferred_element_type=jnp.float32)


def kernel(
    sizes, group, q_in, k_in, v_in, g_in, decay_in_ref, next_ref, gq_ref, gk_ref, gv_ref,
    q_ref, k_ref, v_ref, g_ref, decay_ref, cum, state, grad_state, weighted, weighted_grad, q_dec, k_dec, decay_in, decay_out, columns,
    prefix, suffix, up, down, attn,
    in_sem, decay_sem, prefix_sem, suffix_sem, up_sem, down_sem, attn_sem, next_sem, ready,
):
    seq_count, pipe_count, exp_count = sizes
    seq, pipe, exp = lax.axis_index("seq"), lax.axis_index("pipe"), lax.axis_index("exp")
    heads, rows, dim = q_ref.shape
    groups = heads // group
    hold = min(HOLD, groups - 1)
    part_rows = rows // exp_count
    has_below, has_above = seq > 0, seq < seq_count - 1
    receives, sends = pipe > 0, pipe < pipe_count - 1
    even = pipe % 2 == 0
    upper = 2 * seq >= seq_count

    decay_copy = pltpu.make_async_copy(decay_in_ref, decay_ref, decay_sem)
    decay_copy.start()

    barrier = pltpu.get_barrier_semaphore()

    def greet(condition, device):
        @pl.when(condition)
        def _():
            pl.semaphore_signal(barrier, inc=1, device_id=device, device_id_type=MESH)

    greet(has_below, {"seq": seq - 1})
    greet(has_above, {"seq": seq + 1})
    for other in range(exp_count):
        greet(even & receives, {"pipe": pipe - 1, "exp": other})
        greet(even & sends, {"pipe": pipe + 1, "exp": other})

    key_side, query_side = ((k_in, k_ref), (v_in, v_ref)), ((q_in, q_ref), (g_in, g_ref))

    def in_copies(pairs, at, unit):
        side = 0 if pairs is key_side else 2
        return [pltpu.make_async_copy(src.at[at], dst.at[at], in_sem.at[side + i, unit]) for i, (src, dst) in enumerate(pairs)]

    def head_copies(pairs, h):
        return in_copies(pairs, pl.ds(h, 1), h)

    def group_copies(pairs, t):
        return in_copies(pairs, pl.ds(t * group, group), group - 1 + t)

    def load(*sides):
        for pairs in sides:
            for h in range(group):
                for copy in head_copies(pairs, h):
                    copy.start()
            for t in range(1, groups):
                for copy in group_copies(pairs, t):
                    copy.start()

    @pl.when(upper)
    def _():
        load(query_side, key_side)

    @pl.when(jnp.logical_not(upper))
    def _():
        load(key_side, query_side)

    def enter_kernel():
        beside = has_below.astype(jnp.int32) + has_above.astype(jnp.int32)
        relayed = receives.astype(jnp.int32) + sends.astype(jnp.int32)

        @pl.when(even)
        def _():
            pl.semaphore_wait(barrier, beside)

        @pl.when(jnp.logical_not(even))
        def _():
            pl.semaphore_wait(barrier, beside + exp_count * relayed)
            for other in range(exp_count):
                pl.semaphore_signal(ready, inc=1, device_id={"pipe": pipe - 1, "exp": other}, device_id_type=MESH)

    @pl.when(jnp.logical_not(has_below))
    def _():
        prefix[...] = jnp.zeros_like(prefix)

    @pl.when(jnp.logical_not(has_above))
    def _():
        suffix[...] = jnp.zeros_like(suffix)

    @pl.when(jnp.logical_not(receives))
    def _():
        next_ref[...] = jnp.zeros_like(next_ref)

    decay_copy.wait()
    total = decay_ref[...]
    lane = lax.broadcasted_iota(jnp.int32, total.shape, 1)
    step = 1
    while step < rows:
        total = total + jnp.where(lane >= step, pltpu.roll(total, step, 1), 0.0)
        step *= 2
    cum[...] = total

    def up_copy(h):
        return pltpu.make_async_remote_copy(
            src_ref=up.at[h], dst_ref=prefix.at[h], send_sem=up_sem, recv_sem=prefix_sem.at[h],
            device_id={"seq": seq + 1}, device_id_type=MESH)

    def down_copy(h):
        return pltpu.make_async_remote_copy(
            src_ref=down.at[h], dst_ref=suffix.at[h], send_sem=down_sem, recv_sem=suffix_sem.at[h],
            device_id={"seq": seq - 1}, device_id_type=MESH)

    def attn_copy(head, other):
        place = pl.ds(pl.multiple_of((exp * heads + head) * dim, dim), dim)
        return pltpu.make_async_remote_copy(
            src_ref=attn.at[head, pl.ds(other * part_rows, part_rows)], dst_ref=next_ref.at[:, place],
            send_sem=attn_sem, recv_sem=next_sem,
            device_id={"pipe": pipe + 1, "exp": other}, device_id_type=MESH)

    def decays(h):
        down_rows = jnp.broadcast_to(cum[pl.ds(h, 1), :], (rows, rows)).T
        enter = jnp.exp(down_rows)
        leave = jnp.exp(down_rows[rows - 1:, :] - down_rows)
        decay_in[h], decay_out[h], columns[h] = enter, leave, down_rows

    def from_keys(h, summed):
        kd = (k_ref[h].astype(jnp.float32) * decay_out[h, :, :dim]).astype(jnp.bfloat16)
        k_dec[h] = kd
        if summed:
            own = dot(kd, v_ref[h], (0, 0))
            state[h], up[h] = own, own.astype(jnp.bfloat16)

    def from_queries(h, summed):
        qd = (q_ref[h].astype(jnp.float32) * decay_in[h, :, :dim]).astype(jnp.bfloat16)
        q_dec[h] = qd
        if summed:
            own = dot(qd, g_ref[h], (0, 0))
            grad_state[h], down[h] = own, own.astype(jnp.bfloat16)

    def end_device(condition, pairs, summed, other_pairs, plain, copy_of):
        def one(h):
            decays(h)
            summed(h, True)

        @pl.when(condition)
        def _():
            for copy in head_copies(pairs, 0):
                copy.wait()
            one(0)
            enter_kernel()

            @pl.when(even)
            def _():
                copy_of(0).start()

            @pl.loop(1, group)
            def _(h):
                for copy in head_copies(pairs, h):
                    copy.wait()
                one(h)

                @pl.when(even)
                def _():
                    copy_of(h).start()

            @pl.loop(1, groups)
            def _(t):
                for copy in group_copies(pairs, t):
                    copy.wait()
                for i in range(group):
                    one(t * group + i)

                @pl.when(jnp.logical_not(even) & (t == hold))
                def _():
                    @pl.loop(0, hold * group)
                    def _(h):
                        copy_of(h).start()

                @pl.when(even | (t >= hold))
                def _():
                    for i in range(group):
                        copy_of(t * group + i).start()

            for h in range(group):
                for copy in head_copies(other_pairs, h):
                    copy.wait()
            for t in range(1, groups):
                for copy in group_copies(other_pairs, t):
                    copy.wait()

            @pl.loop(0, groups)
            def _(t):
                for i in range(group):
                    plain(t * group + i, False)

    def middle_device():
        def both(t):
            for i in range(group):
                h = t * group + i
                decays(h)
                from_keys(h, True)
                from_queries(h, True)

        @pl.when(has_below & has_above)
        def _():
            for pairs in (key_side, query_side):
                for h in range(group):
                    for copy in head_copies(pairs, h):
                        copy.wait()
            both(0)
            enter_kernel()

            @pl.loop(1, groups)
            def _(t):
                for pairs in (key_side, query_side):
                    for copy in group_copies(pairs, t):
                        copy.wait()
                both(t)

    def within(first):
        causal = lax.broadcasted_iota(jnp.int32, (rows, rows), 0) >= lax.broadcasted_iota(jnp.int32, (rows, rows), 1)
        for i in range(group):
            h = first * group + i
            weight = jnp.exp(jnp.where(causal, columns[h] - cum[pl.ds(h, 1), :], -1e30))
            weighted[h] = (dot(q_ref[h], k_ref[h], (1, 1)) * weight).astype(jnp.bfloat16)
            weighted_grad[h] = (dot(g_ref[h], v_ref[h], (1, 1)) * weight).astype(jnp.bfloat16)

    def forward(h):
        @pl.when(has_below)
        def _():
            up_copy(h).wait_recv()

            @pl.when(has_above)
            def _():
                gain = decay_in[h, rows - 1:, :]
                up[h] = (gain * prefix[h].astype(jnp.float32) + state[h]).astype(jnp.bfloat16)
                up_copy(h).start()

    def backward(h):
        @pl.when(has_above)
        def _():
            down_copy(h).wait_recv()

            @pl.when(has_below)
            def _():
                gain = decay_in[h, rows - 1:, :]
                down[h] = (gain * suffix[h].astype(jnp.float32) + grad_state[h]).astype(jnp.bfloat16)
                down_copy(h).start()

    def finish_forward(h):
        low = prefix[h]
        out = dot(weighted[h], v_ref[h], (1, 0)) + dot(q_dec[h], low, (1, 0))
        attn[h] = out.astype(jnp.bfloat16)
        gq = dot(weighted_grad[h], k_ref[h], (1, 0)) + dot(g_ref[h], low, (1, 1)) * decay_in[h]
        gq_ref[h] = gq.astype(jnp.bfloat16)

    def send_out(h):
        @pl.when(sends)
        def _():
            for other in range(exp_count):
                attn_copy(h, other).start()

    def finish_backward(h):
        low = suffix[h]
        gk = dot(weighted_grad[h], q_ref[h], (0, 0)) + dot(v_ref[h], low, (1, 1)) * decay_out[h]
        gk_ref[h] = gk.astype(jnp.bfloat16)
        gv = dot(weighted[h], g_ref[h], (0, 0)) + dot(k_dec[h], low, (1, 0))
        gv_ref[h] = gv.astype(jnp.bfloat16)

    end_device(jnp.logical_not(has_below), key_side, from_keys, query_side, from_queries, up_copy)
    end_device(has_below & jnp.logical_not(has_above), query_side, from_queries, key_side, from_keys, down_copy)
    middle_device()

    @pl.loop(0, groups)
    def _(t):
        within(t)

    @pl.when(even & sends)
    def _():
        pl.semaphore_wait(ready, exp_count)

    @pl.loop(0, heads + LAG * (seq_count - 1))
    def _(t):
        ahead = t - LAG * seq
        behind = t - LAG * (seq_count - 1 - seq)
        moves_up = (ahead >= 0) & (ahead < heads)
        moves_down = (behind >= 0) & (behind < heads)

        @pl.when(moves_up)
        def _():
            forward(ahead)

        @pl.when(moves_down)
        def _():
            backward(behind)

        @pl.when(moves_up & moves_down)
        def _():
            finish_forward(ahead)
            finish_backward(behind)

        @pl.when(moves_up & jnp.logical_not(moves_down))
        def _():
            finish_forward(ahead)

        @pl.when(moves_down & jnp.logical_not(moves_up))
        def _():
            finish_backward(behind)

        @pl.when(moves_up)
        def _():
            send_out(ahead)

    @pl.when(has_above)
    def _():
        pltpu.make_async_copy(up, up, up_sem).wait()

    @pl.when(has_below)
    def _():
        pltpu.make_async_copy(down, down, down_sem).wait()

    @pl.when(sends)
    def _():
        pltpu.make_async_copy(attn, attn, attn_sem).wait()

    @pl.when(receives)
    def _():
        pltpu.make_async_copy(next_ref, next_ref, next_sem).wait()


def store(*refs):
    sem = refs[8]
    copies = [pltpu.make_async_copy(refs[i], refs[4 + i], sem.at[i]) for i in range(4)]
    for copy in copies:
        copy.start()
    for copy in copies:
        copy.wait()


def body(sizes, queries, keys, values, grad_out, log_decay):
    seq_count, pipe_count, exp_count = sizes
    _, heads, rows, dim = queries.shape
    group = math.gcd(GROUP, heads)
    low = jax.ShapeDtypeStruct((heads, rows, dim), jnp.bfloat16)
    vmem = pl.BlockSpec(memory_space=pltpu.VMEM)
    low_buf = pltpu.VMEM((heads, rows, dim), jnp.bfloat16)
    state_low = pltpu.VMEM((heads, dim, dim), jnp.bfloat16)
    state_wide = pltpu.VMEM((heads, dim, dim), jnp.float32)
    square_low = pltpu.VMEM((heads, rows, rows), jnp.bfloat16)
    square_wide = pltpu.VMEM((heads, rows, rows), jnp.float32)
    dma = pltpu.SemaphoreType.DMA
    any_place = pl.BlockSpec(memory_space=pl.ANY)
    next_rows = (rows // exp_count, exp_count * heads * dim)
    outs = pl.pallas_call(
        functools.partial(kernel, sizes, group),
        out_shape=(pltpu.VMEM(next_rows, jnp.bfloat16), low_buf, low_buf, low_buf),
        in_specs=[pl.BlockSpec(memory_space=pltpu.HBM)] * 5,
        out_specs=(vmem,) * 4,
        scratch_shapes=[
            low_buf, low_buf, low_buf, low_buf, pltpu.VMEM((heads, rows), jnp.float32),
            pltpu.VMEM((heads, rows), jnp.float32), state_wide, state_wide, square_low, square_low,
            low_buf, low_buf, square_wide, square_wide, square_wide,
            state_low, state_low, state_low, state_low, low_buf,
            dma((4, group - 1 + heads // group)), dma, dma((heads,)), dma((heads,)), dma, dma, dma, dma, pltpu.SemaphoreType.REGULAR,
        ],
        compiler_params=pltpu.CompilerParams(collective_id=0, has_side_effects=True, vmem_limit_bytes=VMEM_LIMIT),
    )(*(pltpu.with_memory_space_constraint(part[0], pltpu.HBM) for part in (queries, keys, values, grad_out, log_decay)))
    outs = pl.pallas_call(
        store,
        out_shape=(jax.ShapeDtypeStruct(next_rows, jnp.bfloat16), low, low, low),
        in_specs=[any_place] * 4,
        out_specs=(any_place,) * 4,
        scratch_shapes=[dma((4,))],
        compiler_params=pltpu.CompilerParams(vmem_limit_bytes=2**20),
    )(*outs)
    return tuple(out[None] for out in outs)


def solution(mesh):
    placed = P("pipe", "exp", "seq", None)
    sizes = tuple(mesh.shape[axis] for axis in ("seq", "pipe", "exp"))
    return jax.shard_map(
        functools.partial(body, sizes),
        mesh=mesh,
        in_specs=(placed, placed, placed, placed, P("pipe", "exp", "seq")),
        out_specs=(P("pipe", ("seq", "exp"), None), placed, placed, placed),
        check_vma=False,
    )
```

```python
import functools
import math

import jax
import jax.numpy as jnp
from jax import lax
from jax.experimental import pallas as pl
from jax.experimental.pallas import tpu as pltpu
from jax.sharding import PartitionSpec as P

MESH = pl.DeviceIdType.MESH
LAG = 5
GROUP = 4
HOLD = 2
VMEM_LIMIT = 61 * 2**20


def dot(left, right, dims):
    return lax.dot_general(left, right, ((dims[:1], dims[1:]), ((), ())), preferred_element_type=jnp.float32)


def kernel(
    sizes, group, q_in, k_in, v_in, g_in, decay_in_ref, next_ref, gq_ref, gk_ref, gv_ref,
    q_ref, k_ref, v_ref, g_ref, decay_ref, cum, enter_rows, leave_rows, gains, state, grad_state, q_dec, k_dec, decay_in, decay_out,
    weighted, weighted_grad,
    prefix, suffix, up, down, attn,
    in_sem, decay_sem, prefix_sem, suffix_sem, up_sem, down_sem, attn_sem, next_sem, ready,
):
    seq_count, pipe_count, exp_count = sizes
    seq, pipe, exp = lax.axis_index("seq"), lax.axis_index("pipe"), lax.axis_index("exp")
    heads, rows, dim = q_ref.shape
    groups = heads // group
    hold = min(HOLD, groups - 1)
    part_rows = rows // exp_count
    has_below, has_above = seq > 0, seq < seq_count - 1
    receives, sends = pipe > 0, pipe < pipe_count - 1
    even = pipe % 2 == 0
    upper = 2 * seq >= seq_count

    decay_copy = pltpu.make_async_copy(decay_in_ref, decay_ref, decay_sem)
    decay_copy.start()

    barrier = pltpu.get_barrier_semaphore()

    def greet(condition, device):
        @pl.when(condition)
        def _():
            pl.semaphore_signal(barrier, inc=1, device_id=device, device_id_type=MESH)

    greet(has_below, {"seq": seq - 1})
    greet(has_above, {"seq": seq + 1})
    for other in range(exp_count):
        greet(even & receives, {"pipe": pipe - 1, "exp": other})
        greet(even & sends, {"pipe": pipe + 1, "exp": other})

    key_side, query_side = ((k_in, k_ref), (v_in, v_ref)), ((q_in, q_ref), (g_in, g_ref))

    def pieces(pairs, piece):
        side = 0 if pairs is key_side else 2
        at = pl.ds(1, heads - 1) if piece else pl.ds(0, 1)
        return [pltpu.make_async_copy(src.at[at], dst.at[at], in_sem.at[side + i, piece]) for i, (src, dst) in enumerate(pairs)]

    def load(*sides):
        for pairs in sides:
            for piece in range(2):
                for copy in pieces(pairs, piece):
                    copy.start()

    @pl.when(upper)
    def _():
        load(query_side, key_side)

    @pl.when(jnp.logical_not(upper))
    def _():
        load(key_side, query_side)

    def enter_kernel():
        beside = has_below.astype(jnp.int32) + has_above.astype(jnp.int32)
        relayed = receives.astype(jnp.int32) + sends.astype(jnp.int32)

        @pl.when(even)
        def _():
            pl.semaphore_wait(barrier, beside)

        @pl.when(jnp.logical_not(even))
        def _():
            pl.semaphore_wait(barrier, beside + exp_count * relayed)
            for other in range(exp_count):
                pl.semaphore_signal(ready, inc=1, device_id={"pipe": pipe - 1, "exp": other}, device_id_type=MESH)

    @pl.when(jnp.logical_not(has_below))
    def _():
        prefix[...] = jnp.zeros_like(prefix)

    @pl.when(jnp.logical_not(has_above))
    def _():
        suffix[...] = jnp.zeros_like(suffix)

    @pl.when(jnp.logical_not(receives))
    def _():
        next_ref[...] = jnp.zeros_like(next_ref)

    decay_copy.wait()
    rates, parts = decay_ref[...], []
    for _ in range(3):
        parts.append(rates.astype(jnp.bfloat16))
        rates = rates - parts[-1].astype(jnp.float32)
    upto = lax.broadcasted_iota(jnp.int32, (rows, rows), 0) <= lax.broadcasted_iota(jnp.int32, (rows, rows), 1)
    ones = jnp.where(upto, 1.0, 0.0).astype(jnp.bfloat16)
    total = dot(parts[2], ones, (1, 0)) + dot(parts[1], ones, (1, 0)) + dot(parts[0], ones, (1, 0))
    last = total[:, rows - 1:]
    cum[...] = total
    enter_rows[...] = jnp.exp(total)
    leave_rows[...] = jnp.exp(last - total)
    gains[...] = jnp.broadcast_to(jnp.exp(last), gains.shape)

    def up_copy(h):
        return pltpu.make_async_remote_copy(
            src_ref=up.at[h], dst_ref=prefix.at[h], send_sem=up_sem, recv_sem=prefix_sem.at[h],
            device_id={"seq": seq + 1}, device_id_type=MESH)

    def down_copy(h):
        return pltpu.make_async_remote_copy(
            src_ref=down.at[h], dst_ref=suffix.at[h], send_sem=down_sem, recv_sem=suffix_sem.at[h],
            device_id={"seq": seq - 1}, device_id_type=MESH)

    def attn_copy(head, other):
        place = pl.ds(pl.multiple_of((exp * heads + head) * dim, dim), dim)
        return pltpu.make_async_remote_copy(
            src_ref=attn.at[head, pl.ds(other * part_rows, part_rows)], dst_ref=next_ref.at[:, place],
            send_sem=attn_sem, recv_sem=next_sem,
            device_id={"pipe": pipe + 1, "exp": other}, device_id_type=MESH)

    def scaled(ref, decay_rows, h):
        return (ref[h].T.astype(jnp.float32) * decay_rows[pl.ds(h, 1), :]).astype(jnp.bfloat16)

    def from_keys(h):
        own = dot(scaled(k_ref, leave_rows, h), v_ref[h], (1, 0))
        state[h], up[h] = own, own.astype(jnp.bfloat16)

    def from_queries(h):
        own = dot(scaled(q_ref, enter_rows, h), g_ref[h], (1, 0))
        grad_state[h], down[h] = own, own.astype(jnp.bfloat16)

    def end_device(condition, pairs, one, other_pairs, copy_of):
        @pl.when(condition)
        def _():
            for copy in pieces(pairs, 0):
                copy.wait()
            one(0)
            enter_kernel()

            @pl.when(even)
            def _():
                copy_of(0).start()

            for copy in pieces(pairs, 1):
                copy.wait()
            for h in range(1, group):
                one(h)

            @pl.when(even)
            def _():
                for h in range(1, group):
                    copy_of(h).start()

            @pl.loop(1, groups)
            def _(t):
                for i in range(group):
                    one(t * group + i)

                @pl.when(jnp.logical_not(even) & (t == hold))
                def _():
                    @pl.loop(0, hold * group)
                    def _(h):
                        copy_of(h).start()

                @pl.when(even | (t >= hold))
                def _():
                    for i in range(group):
                        copy_of(t * group + i).start()

            for piece in range(2):
                for copy in pieces(other_pairs, piece):
                    copy.wait()

    def middle_device():
        @pl.when(has_below & has_above)
        def _():
            for pairs in (key_side, query_side):
                for piece in range(2):
                    for copy in pieces(pairs, piece):
                        copy.wait()
            enter_kernel()

            @pl.loop(0, groups)
            def _(t):
                for i in range(group):
                    h = t * group + i
                    from_keys(h)
                    from_queries(h)

    def within(first):
        causal = lax.broadcasted_iota(jnp.int32, (rows, rows), 0) >= lax.broadcasted_iota(jnp.int32, (rows, rows), 1)
        for i in range(group):
            h = first * group + i
            along = jnp.broadcast_to(cum[pl.ds(h, 1), :], (rows, rows))
            down_rows = along.T
            enter = jnp.exp(down_rows[:, :dim])
            leave = jnp.exp(down_rows[rows - 1:, :dim] - down_rows[:, :dim])
            decay_in[h], decay_out[h] = enter, leave
            q, k, v, g = q_ref[h], k_ref[h], v_ref[h], g_ref[h]
            q_dec[h] = (q.astype(jnp.float32) * enter).astype(jnp.bfloat16)
            k_dec[h] = (k.astype(jnp.float32) * leave).astype(jnp.bfloat16)
            weight = jnp.exp(jnp.where(causal, down_rows - along, -1e30))
            weighted[h] = (dot(q, k, (1, 1)) * weight).astype(jnp.bfloat16)
            weighted_grad[h] = (dot(g, v, (1, 1)) * weight).astype(jnp.bfloat16)

    def forward(h):
        @pl.when(has_below)
        def _():
            up_copy(h).wait_recv()

            @pl.when(has_above)
            def _():
                gain = gains[pl.ds(h, 1), :]
                up[h] = (gain * prefix[h].astype(jnp.float32) + state[h]).astype(jnp.bfloat16)
                up_copy(h).start()

    def backward(h):
        @pl.when(has_above)
        def _():
            down_copy(h).wait_recv()

            @pl.when(has_below)
            def _():
                gain = gains[pl.ds(h, 1), :]
                down[h] = (gain * suffix[h].astype(jnp.float32) + grad_state[h]).astype(jnp.bfloat16)
                down_copy(h).start()

    def finish_out(h):
        attn[h] = (dot(weighted[h], v_ref[h], (1, 0)) + dot(q_dec[h], prefix[h], (1, 0))).astype(jnp.bfloat16)

    def finish_queries(h):
        gq_ref[h] = (dot(weighted_grad[h], k_ref[h], (1, 0)) + dot(g_ref[h], prefix[h], (1, 1)) * decay_in[h]).astype(jnp.bfloat16)

    def send_out(h):
        @pl.when(sends)
        def _():
            for other in range(exp_count):
                attn_copy(h, other).start()

    def finish_backward(h):
        low = suffix[h]
        gk_ref[h] = (dot(weighted_grad[h], q_ref[h], (0, 0)) + dot(v_ref[h], low, (1, 1)) * decay_out[h]).astype(jnp.bfloat16)
        gv_ref[h] = (dot(weighted[h], g_ref[h], (0, 0)) + dot(k_dec[h], low, (1, 0))).astype(jnp.bfloat16)

    end_device(jnp.logical_not(has_below), key_side, from_keys, query_side, up_copy)
    end_device(has_below & jnp.logical_not(has_above), query_side, from_queries, key_side, down_copy)
    middle_device()

    @pl.loop(0, groups)
    def _(t):
        within(t)

    @pl.when(even & sends)
    def _():
        pl.semaphore_wait(ready, exp_count)

    @pl.loop(0, heads + LAG * (seq_count - 1))
    def _(t):
        ahead = t - LAG * seq
        behind = t - LAG * (seq_count - 1 - seq)
        moves_up = (ahead >= 0) & (ahead < heads)
        moves_down = (behind >= 0) & (behind < heads)

        @pl.when(moves_up)
        def _():
            forward(ahead)

        @pl.when(moves_down)
        def _():
            backward(behind)

        @pl.when(moves_up & moves_down)
        def _():
            finish_out(ahead)
            finish_queries(ahead)
            finish_backward(behind)
            send_out(ahead)

        @pl.when(moves_up & jnp.logical_not(moves_down))
        def _():
            finish_out(ahead)
            send_out(ahead)
            finish_queries(ahead)

        @pl.when(moves_down & jnp.logical_not(moves_up))
        def _():
            finish_backward(behind)

    @pl.when(has_above)
    def _():
        pltpu.make_async_copy(up, up, up_sem).wait()

    @pl.when(has_below)
    def _():
        pltpu.make_async_copy(down, down, down_sem).wait()

    @pl.when(sends)
    def _():
        pltpu.make_async_copy(attn, attn, attn_sem).wait()

    @pl.when(receives)
    def _():
        pltpu.make_async_copy(next_ref, next_ref, next_sem).wait()


def store(*refs):
    sem = refs[8]
    copies = [pltpu.make_async_copy(refs[i], refs[4 + i], sem.at[i]) for i in range(4)]
    for copy in copies:
        copy.start()
    for copy in copies:
        copy.wait()


def body(sizes, queries, keys, values, grad_out, log_decay):
    seq_count, pipe_count, exp_count = sizes
    _, heads, rows, dim = queries.shape
    group = math.gcd(GROUP, heads)
    low = jax.ShapeDtypeStruct((heads, rows, dim), jnp.bfloat16)
    vmem = pl.BlockSpec(memory_space=pltpu.VMEM)
    low_buf = pltpu.VMEM((heads, rows, dim), jnp.bfloat16)
    state_low = pltpu.VMEM((heads, dim, dim), jnp.bfloat16)
    state_wide = pltpu.VMEM((heads, dim, dim), jnp.float32)
    square_low = pltpu.VMEM((heads, rows, rows), jnp.bfloat16)
    wide = pltpu.VMEM((heads, rows, dim), jnp.float32)
    by_row = pltpu.VMEM((heads, rows), jnp.float32)
    dma = pltpu.SemaphoreType.DMA
    any_place = pl.BlockSpec(memory_space=pl.ANY)
    next_rows = (rows // exp_count, exp_count * heads * dim)
    outs = pl.pallas_call(
        functools.partial(kernel, sizes, group),
        out_shape=(pltpu.VMEM(next_rows, jnp.bfloat16), low_buf, low_buf, low_buf),
        in_specs=[pl.BlockSpec(memory_space=pltpu.HBM)] * 5,
        out_specs=(vmem,) * 4,
        scratch_shapes=[
            low_buf, low_buf, low_buf, low_buf, by_row, by_row, by_row, by_row, pltpu.VMEM((heads, dim), jnp.float32),
            state_wide, state_wide, low_buf, low_buf, wide, wide, square_low, square_low,
            state_low, state_low, state_low, state_low, low_buf,
            dma((4, 2)), dma, dma((heads,)), dma((heads,)), dma, dma, dma, dma, pltpu.SemaphoreType.REGULAR,
        ],
        compiler_params=pltpu.CompilerParams(collective_id=0, has_side_effects=True, vmem_limit_bytes=VMEM_LIMIT),
    )(*(pltpu.with_memory_space_constraint(part[0], pltpu.HBM) for part in (queries, keys, values, grad_out, log_decay)))
    outs = pl.pallas_call(
        store,
        out_shape=(jax.ShapeDtypeStruct(next_rows, jnp.bfloat16), low, low, low),
        in_specs=[any_place] * 4,
        out_specs=(any_place,) * 4,
        scratch_shapes=[dma((4,))],
        compiler_params=pltpu.CompilerParams(vmem_limit_bytes=2**20),
    )(*outs)
    return tuple(out[None] for out in outs)


def solution(mesh):
    placed = P("pipe", "exp", "seq", None)
    sizes = tuple(mesh.shape[axis] for axis in ("seq", "pipe", "exp"))
    return jax.shard_map(
        functools.partial(body, sizes),
        mesh=mesh,
        in_specs=(placed, placed, placed, placed, P("pipe", "exp", "seq")),
        out_specs=(P("pipe", ("seq", "exp"), None), placed, placed, placed),
        check_vma=False,
    )
```

```python
import functools
import math

import jax
import jax.numpy as jnp
from jax import lax
from jax.experimental import pallas as pl
from jax.experimental.pallas import tpu as pltpu
from jax.sharding import PartitionSpec as P

MESH = pl.DeviceIdType.MESH
DOWN_LAG = 16
UP_LAG = 14
LAG_UNIT = 3
GROUP = 4
HOLD = 3
VMEM_LIMIT = 61 * 2**20


def dot(left, right, dims):
    return lax.dot_general(left, right, ((dims[:1], dims[1:]), ((), ())), preferred_element_type=jnp.float32)


def kernel(
    sizes, group, q_in, k_in, v_in, g_in, decay_in_ref, next_ref, gq_ref, gk_ref, gv_ref,
    q_ref, k_ref, v_ref, g_ref, decay_ref, cum, enter_rows, leave_rows, gains, state, grad_state, q_dec, k_dec, decay_in, decay_out,
    weighted, weighted_grad,
    prefix, suffix, up, down, attn,
    in_sem, decay_sem, prefix_sem, suffix_sem, up_sem, down_sem, attn_sem, next_sem, ready,
):
    seq_count, pipe_count, exp_count = sizes
    seq, pipe, exp = lax.axis_index("seq"), lax.axis_index("pipe"), lax.axis_index("exp")
    heads, rows, dim = q_ref.shape
    groups = heads // group
    hold = min(HOLD, groups - 1)
    part_rows = rows // exp_count
    has_below, has_above = seq > 0, seq < seq_count - 1
    receives, sends = pipe > 0, pipe < pipe_count - 1
    even = pipe % 2 == 0
    upper = 2 * seq >= seq_count

    decay_copy = pltpu.make_async_copy(decay_in_ref, decay_ref, decay_sem)
    decay_copy.start()

    barrier = pltpu.get_barrier_semaphore()

    def greet(condition, device):
        @pl.when(condition)
        def _():
            pl.semaphore_signal(barrier, inc=1, device_id=device, device_id_type=MESH)

    greet(has_below, {"seq": seq - 1})
    greet(has_above, {"seq": seq + 1})
    for other in range(exp_count):
        greet(even & receives, {"pipe": pipe - 1, "exp": other})
        greet(even & sends, {"pipe": pipe + 1, "exp": other})

    key_side, query_side = ((k_in, k_ref), (v_in, v_ref)), ((q_in, q_ref), (g_in, g_ref))

    def pieces(pairs, piece):
        side = 0 if pairs is key_side else 2
        at = pl.ds(1, heads - 1) if piece else pl.ds(0, 1)
        return [pltpu.make_async_copy(src.at[at], dst.at[at], in_sem.at[side + i, piece]) for i, (src, dst) in enumerate(pairs)]

    def load(*sides):
        for pairs in sides:
            for piece in range(2):
                for copy in pieces(pairs, piece):
                    copy.start()

    @pl.when(upper)
    def _():
        load(query_side, key_side)

    @pl.when(jnp.logical_not(upper))
    def _():
        load(key_side, query_side)

    def enter_kernel():
        beside = has_below.astype(jnp.int32) + has_above.astype(jnp.int32)
        relayed = receives.astype(jnp.int32) + sends.astype(jnp.int32)

        @pl.when(even)
        def _():
            pl.semaphore_wait(barrier, beside)

        @pl.when(jnp.logical_not(even))
        def _():
            pl.semaphore_wait(barrier, beside + exp_count * relayed)
            for other in range(exp_count):
                pl.semaphore_signal(ready, inc=1, device_id={"pipe": pipe - 1, "exp": other}, device_id_type=MESH)

    @pl.when(jnp.logical_not(has_below))
    def _():
        prefix[...] = jnp.zeros_like(prefix)

    @pl.when(jnp.logical_not(has_above))
    def _():
        suffix[...] = jnp.zeros_like(suffix)

    @pl.when(jnp.logical_not(receives))
    def _():
        next_ref[...] = jnp.zeros_like(next_ref)

    decay_copy.wait()
    rates, parts = decay_ref[...], []
    for _ in range(3):
        parts.append(rates.astype(jnp.bfloat16))
        rates = rates - parts[-1].astype(jnp.float32)
    upto = lax.broadcasted_iota(jnp.int32, (rows, rows), 0) <= lax.broadcasted_iota(jnp.int32, (rows, rows), 1)
    ones = jnp.where(upto, 1.0, 0.0).astype(jnp.bfloat16)
    total = dot(parts[2], ones, (1, 0)) + dot(parts[1], ones, (1, 0)) + dot(parts[0], ones, (1, 0))
    last = total[:, rows - 1:]
    cum[...] = total
    enter_rows[...] = jnp.exp(total)
    leave_rows[...] = jnp.exp(last - total)
    gains[...] = jnp.broadcast_to(jnp.exp(last), gains.shape)

    def up_copy(h):
        return pltpu.make_async_remote_copy(
            src_ref=up.at[h], dst_ref=prefix.at[h], send_sem=up_sem, recv_sem=prefix_sem.at[h],
            device_id={"seq": seq + 1}, device_id_type=MESH)

    def down_copy(h):
        return pltpu.make_async_remote_copy(
            src_ref=down.at[h], dst_ref=suffix.at[h], send_sem=down_sem, recv_sem=suffix_sem.at[h],
            device_id={"seq": seq - 1}, device_id_type=MESH)

    def attn_copy(head, other):
        place = pl.ds(pl.multiple_of((exp * heads + head) * dim, dim), dim)
        return pltpu.make_async_remote_copy(
            src_ref=attn.at[head, pl.ds(other * part_rows, part_rows)], dst_ref=next_ref.at[:, place],
            send_sem=attn_sem, recv_sem=next_sem,
            device_id={"pipe": pipe + 1, "exp": other}, device_id_type=MESH)

    def scaled(ref, decay_rows, h):
        return (ref[h].T.astype(jnp.float32) * decay_rows[pl.ds(h, 1), :]).astype(jnp.bfloat16)

    def from_keys(h):
        own = dot(scaled(k_ref, leave_rows, h), v_ref[h], (1, 0))
        state[h], up[h] = own, own.astype(jnp.bfloat16)

    def from_queries(h):
        own = dot(scaled(q_ref, enter_rows, h), g_ref[h], (1, 0))
        grad_state[h], down[h] = own, own.astype(jnp.bfloat16)

    def end_device(condition, pairs, one, other_pairs, copy_of):
        @pl.when(condition)
        def _():
            for copy in pieces(pairs, 0):
                copy.wait()
            one(0)
            enter_kernel()

            @pl.when(even)
            def _():
                copy_of(0).start()

            for copy in pieces(pairs, 1):
                copy.wait()
            for h in range(1, group):
                one(h)

            @pl.when(even)
            def _():
                for h in range(1, group):
                    copy_of(h).start()

            @pl.loop(1, groups)
            def _(t):
                for i in range(group):
                    one(t * group + i)

                @pl.when(jnp.logical_not(even) & (t == hold))
                def _():
                    @pl.loop(0, hold * group)
                    def _(h):
                        copy_of(h).start()

                @pl.when(even | (t >= hold))
                def _():
                    for i in range(group):
                        copy_of(t * group + i).start()

            for piece in range(2):
                for copy in pieces(other_pairs, piece):
                    copy.wait()

    def middle_device():
        @pl.when(has_below & has_above)
        def _():
            for pairs in (key_side, query_side):
                for piece in range(2):
                    for copy in pieces(pairs, piece):
                        copy.wait()
            enter_kernel()

            @pl.loop(0, groups)
            def _(t):
                for i in range(group):
                    h = t * group + i
                    from_keys(h)
                    from_queries(h)

    def within(first):
        causal = lax.broadcasted_iota(jnp.int32, (rows, rows), 0) >= lax.broadcasted_iota(jnp.int32, (rows, rows), 1)
        for i in range(group):
            h = first * group + i
            along = jnp.broadcast_to(cum[pl.ds(h, 1), :], (rows, rows))
            down_rows = along.T
            enter = jnp.exp(down_rows[:, :dim])
            leave = jnp.exp(down_rows[rows - 1:, :dim] - down_rows[:, :dim])
            decay_in[h], decay_out[h] = enter, leave
            q, k, v, g = q_ref[h], k_ref[h], v_ref[h], g_ref[h]
            q_dec[h] = (q.astype(jnp.float32) * enter).astype(jnp.bfloat16)
            k_dec[h] = (k.astype(jnp.float32) * leave).astype(jnp.bfloat16)
            weight = jnp.exp(jnp.where(causal, down_rows - along, -1e30))
            weighted[h] = (dot(q, k, (1, 1)) * weight).astype(jnp.bfloat16)
            weighted_grad[h] = (dot(g, v, (1, 1)) * weight).astype(jnp.bfloat16)

    def forward(h):
        @pl.when(has_below)
        def _():
            up_copy(h).wait_recv()

            @pl.when(has_above)
            def _():
                gain = gains[pl.ds(h, 1), :]
                up[h] = (gain * prefix[h].astype(jnp.float32) + state[h]).astype(jnp.bfloat16)
                up_copy(h).start()

    def backward(h):
        @pl.when(has_above)
        def _():
            down_copy(h).wait_recv()

            @pl.when(has_below)
            def _():
                gain = gains[pl.ds(h, 1), :]
                down[h] = (gain * suffix[h].astype(jnp.float32) + grad_state[h]).astype(jnp.bfloat16)
                down_copy(h).start()

    def finish_out(h):
        attn[h] = (dot(weighted[h], v_ref[h], (1, 0)) + dot(q_dec[h], prefix[h], (1, 0))).astype(jnp.bfloat16)

    def finish_queries(h):
        gq_ref[h] = (dot(weighted_grad[h], k_ref[h], (1, 0)) + dot(g_ref[h], prefix[h], (1, 1)) * decay_in[h]).astype(jnp.bfloat16)

    def send_out(h):
        @pl.when(sends)
        def _():
            for other in range(exp_count):
                attn_copy(h, other).start()

    def finish_backward(h):
        low = suffix[h]
        gk_ref[h] = (dot(weighted_grad[h], q_ref[h], (0, 0)) + dot(v_ref[h], low, (1, 1)) * decay_out[h]).astype(jnp.bfloat16)
        gv_ref[h] = (dot(weighted[h], g_ref[h], (0, 0)) + dot(k_dec[h], low, (1, 0))).astype(jnp.bfloat16)

    end_device(jnp.logical_not(has_below), key_side, from_keys, query_side, up_copy)
    end_device(has_below & jnp.logical_not(has_above), query_side, from_queries, key_side, down_copy)
    middle_device()

    @pl.loop(0, groups)
    def _(t):
        within(t)

    @pl.when(even & sends)
    def _():
        pl.semaphore_wait(ready, exp_count)

    @pl.loop(0, heads + max(UP_LAG, DOWN_LAG) * (seq_count - 1) // LAG_UNIT)
    def _(t):
        ahead = t - UP_LAG * seq // LAG_UNIT
        behind = t - DOWN_LAG * (seq_count - 1 - seq) // LAG_UNIT
        moves_up = (ahead >= 0) & (ahead < heads)
        moves_down = (behind >= 0) & (behind < heads)

        @pl.when(moves_up)
        def _():
            forward(ahead)

        @pl.when(moves_down)
        def _():
            backward(behind)

        @pl.when(moves_up & moves_down)
        def _():
            finish_out(ahead)
            finish_queries(ahead)
            finish_backward(behind)
            send_out(ahead)

        @pl.when(moves_up & jnp.logical_not(moves_down))
        def _():
            finish_out(ahead)
            send_out(ahead)
            finish_queries(ahead)

        @pl.when(moves_down & jnp.logical_not(moves_up))
        def _():
            finish_backward(behind)

    @pl.when(has_above)
    def _():
        pltpu.make_async_copy(up, up, up_sem).wait()

    @pl.when(has_below)
    def _():
        pltpu.make_async_copy(down, down, down_sem).wait()

    @pl.when(sends)
    def _():
        pltpu.make_async_copy(attn, attn, attn_sem).wait()

    @pl.when(receives)
    def _():
        pltpu.make_async_copy(next_ref, next_ref, next_sem).wait()


def store(*refs):
    sem = refs[8]
    copies = [pltpu.make_async_copy(refs[i], refs[4 + i], sem.at[i]) for i in range(4)]
    for copy in copies:
        copy.start()
    for copy in copies:
        copy.wait()


def body(sizes, queries, keys, values, grad_out, log_decay):
    seq_count, pipe_count, exp_count = sizes
    _, heads, rows, dim = queries.shape
    group = math.gcd(GROUP, heads)
    low = jax.ShapeDtypeStruct((heads, rows, dim), jnp.bfloat16)
    vmem = pl.BlockSpec(memory_space=pltpu.VMEM)
    low_buf = pltpu.VMEM((heads, rows, dim), jnp.bfloat16)
    state_low = pltpu.VMEM((heads, dim, dim), jnp.bfloat16)
    state_wide = pltpu.VMEM((heads, dim, dim), jnp.float32)
    square_low = pltpu.VMEM((heads, rows, rows), jnp.bfloat16)
    wide = pltpu.VMEM((heads, rows, dim), jnp.float32)
    by_row = pltpu.VMEM((heads, rows), jnp.float32)
    dma = pltpu.SemaphoreType.DMA
    any_place = pl.BlockSpec(memory_space=pl.ANY)
    next_rows = (rows // exp_count, exp_count * heads * dim)
    outs = pl.pallas_call(
        functools.partial(kernel, sizes, group),
        out_shape=(pltpu.VMEM(next_rows, jnp.bfloat16), low_buf, low_buf, low_buf),
        in_specs=[pl.BlockSpec(memory_space=pltpu.HBM)] * 5,
        out_specs=(vmem,) * 4,
        scratch_shapes=[
            low_buf, low_buf, low_buf, low_buf, by_row, by_row, by_row, by_row, pltpu.VMEM((heads, dim), jnp.float32),
            state_wide, state_wide, low_buf, low_buf, wide, wide, square_low, square_low,
            state_low, state_low, state_low, state_low, low_buf,
            dma((4, 2)), dma, dma((heads,)), dma((heads,)), dma, dma, dma, dma, pltpu.SemaphoreType.REGULAR,
        ],
        compiler_params=pltpu.CompilerParams(collective_id=0, has_side_effects=True, vmem_limit_bytes=VMEM_LIMIT),
    )(*(pltpu.with_memory_space_constraint(part[0], pltpu.HBM) for part in (queries, keys, values, grad_out, log_decay)))
    outs = pl.pallas_call(
        store,
        out_shape=(jax.ShapeDtypeStruct(next_rows, jnp.bfloat16), low, low, low),
        in_specs=[any_place] * 4,
        out_specs=(any_place,) * 4,
        scratch_shapes=[dma((4,))],
        compiler_params=pltpu.CompilerParams(vmem_limit_bytes=2**20),
    )(*outs)
    return tuple(out[None] for out in outs)


def solution(mesh):
    placed = P("pipe", "exp", "seq", None)
    sizes = tuple(mesh.shape[axis] for axis in ("seq", "pipe", "exp"))
    return jax.shard_map(
        functools.partial(body, sizes),
        mesh=mesh,
        in_specs=(placed, placed, placed, placed, P("pipe", "exp", "seq")),
        out_specs=(P("pipe", ("seq", "exp"), None), placed, placed, placed),
        check_vma=False,
    )
```

```python
import functools
import math

import jax
import jax.numpy as jnp
from jax import lax
from jax.experimental import pallas as pl
from jax.experimental.pallas import tpu as pltpu
from jax.sharding import PartitionSpec as P

MESH = pl.DeviceIdType.MESH
DOWN_LAG = 16
UP_LAG = 14
LAG_UNIT = 3
GROUP = 4
HOLD = 3
VMEM_LIMIT = 61 * 2**20


def dot(left, right, dims):
    return lax.dot_general(left, right, ((dims[:1], dims[1:]), ((), ())), preferred_element_type=jnp.float32)


def kernel(
    sizes, group, q_in, k_in, v_in, g_in, decay_in_ref, next_ref, gq_ref, gk_ref, gv_ref,
    loaded, decay_ref, cum, enter_rows, leave_rows, gains, state, grad_state, q_dec, k_dec, decay_in, decay_out,
    weighted, weighted_grad,
    prefix, suffix, up, down, attn,
    in_sem, decay_sem, prefix_sem, suffix_sem, up_sem, down_sem, attn_sem, next_sem, ready,
):
    seq_count, pipe_count, exp_count = sizes
    seq, pipe, exp = lax.axis_index("seq"), lax.axis_index("pipe"), lax.axis_index("exp")
    k_ref, v_ref, q_ref, g_ref = (loaded.at[i] for i in range(4))
    heads, rows, dim = loaded.shape[1:]
    groups = heads // group
    hold = min(HOLD, groups - 1)
    part_rows = rows // exp_count
    has_below, has_above = seq > 0, seq < seq_count - 1
    middle = has_below & has_above
    receives, sends = pipe > 0, pipe < pipe_count - 1
    even = pipe % 2 == 0
    upper = 2 * seq >= seq_count

    decay_copy = pltpu.make_async_copy(decay_in_ref, decay_ref, decay_sem)
    decay_copy.start()

    barrier = pltpu.get_barrier_semaphore()

    def greet(condition, device):
        @pl.when(condition)
        def _():
            pl.semaphore_signal(barrier, inc=1, device_id=device, device_id_type=MESH)


    key_side, query_side = 0, 1

    def heads_of(piece):
        return pl.ds(1, heads - 1) if piece else pl.ds(0, 1)

    def arrived(side, piece):
        both = loaded.at[pl.ds(2 * side, 2), heads_of(piece)]
        return pltpu.make_async_copy(both, both, in_sem.at[side, piece])

    def load(side, piece):
        for i in range(2):
            src = ((k_in, v_in), (q_in, g_in))[side][i].at[heads_of(piece)]
            pltpu.make_async_copy(src, loaded.at[2 * side + i, heads_of(piece)], in_sem.at[side, piece]).start()

    @pl.when(upper)
    def _():
        load(query_side, 0)

    @pl.when(jnp.logical_not(upper))
    def _():
        load(key_side, 0)

    greet(has_below, {"seq": seq - 1})
    greet(has_above, {"seq": seq + 1})

    for other in range(exp_count):
        greet(even & receives, {"pipe": pipe - 1, "exp": other})
        greet(even & sends, {"pipe": pipe + 1, "exp": other})

    @pl.when(upper)
    def _():
        load(query_side, 1)
        load(key_side, 0)
        load(key_side, 1)

    @pl.when(jnp.logical_not(upper))
    def _():
        load(key_side, 1)
        load(query_side, 0)
        load(query_side, 1)

    def enter_kernel():
        beside = has_below.astype(jnp.int32) + has_above.astype(jnp.int32)
        relayed = receives.astype(jnp.int32) + sends.astype(jnp.int32)

        @pl.when(even)
        def _():
            pl.semaphore_wait(barrier, beside)

        @pl.when(jnp.logical_not(even))
        def _():
            pl.semaphore_wait(barrier, beside + exp_count * relayed)
            for other in range(exp_count):
                pl.semaphore_signal(ready, inc=1, device_id={"pipe": pipe - 1, "exp": other}, device_id_type=MESH)

    @pl.when(jnp.logical_not(has_below))
    def _():
        prefix[...] = jnp.zeros_like(prefix)

    @pl.when(jnp.logical_not(has_above))
    def _():
        suffix[...] = jnp.zeros_like(suffix)

    @pl.when(jnp.logical_not(receives))
    def _():
        next_ref[...] = jnp.zeros_like(next_ref)

    decay_copy.wait()
    rates, parts = decay_ref[...], []
    for _ in range(3):
        parts.append(rates.astype(jnp.bfloat16))
        rates = rates - parts[-1].astype(jnp.float32)
    upto = lax.broadcasted_iota(jnp.int32, (rows, rows), 0) <= lax.broadcasted_iota(jnp.int32, (rows, rows), 1)
    ones = jnp.where(upto, 1.0, 0.0).astype(jnp.bfloat16)
    total = dot(parts[2], ones, (1, 0)) + dot(parts[1], ones, (1, 0)) + dot(parts[0], ones, (1, 0))
    last = total[:, rows - 1:]
    cum[...] = total
    enter_rows[...] = jnp.exp(total)
    leave_rows[...] = jnp.exp(last - total)
    gains[...] = jnp.broadcast_to(jnp.exp(last), gains.shape)

    def up_copy(h):
        return pltpu.make_async_remote_copy(
            src_ref=up.at[h], dst_ref=prefix.at[h], send_sem=up_sem, recv_sem=prefix_sem.at[h],
            device_id={"seq": seq + 1}, device_id_type=MESH)

    def down_copy(h):
        return pltpu.make_async_remote_copy(
            src_ref=down.at[h], dst_ref=suffix.at[h], send_sem=down_sem, recv_sem=suffix_sem.at[h],
            device_id={"seq": seq - 1}, device_id_type=MESH)

    def attn_copy(head, other):
        place = pl.ds(pl.multiple_of((exp * heads + head) * dim, dim), dim)
        return pltpu.make_async_remote_copy(
            src_ref=attn.at[head, pl.ds(other * part_rows, part_rows)], dst_ref=next_ref.at[:, place],
            send_sem=attn_sem, recv_sem=next_sem,
            device_id={"pipe": pipe + 1, "exp": other}, device_id_type=MESH)

    def scaled(ref, decay_rows, h):
        return (ref[h].T.astype(jnp.float32) * decay_rows[pl.ds(h, 1), :]).astype(jnp.bfloat16)

    def from_keys(h):
        own = dot(scaled(k_ref, leave_rows, h), v_ref[h], (1, 0))
        state[h], up[h] = own, own.astype(jnp.bfloat16)

    def from_queries(h):
        own = dot(scaled(q_ref, enter_rows, h), g_ref[h], (1, 0))
        grad_state[h], down[h] = own, own.astype(jnp.bfloat16)

    def end_device(condition, side, one, other_side, copy_of):
        @pl.when(condition)
        def _():
            arrived(side, 0).wait()
            one(0)
            enter_kernel()

            @pl.when(even)
            def _():
                copy_of(0).start()

            arrived(side, 1).wait()
            for h in range(1, group):
                one(h)

            @pl.when(even)
            def _():
                for h in range(1, group):
                    copy_of(h).start()

            @pl.loop(1, groups)
            def _(t):
                for i in range(group):
                    one(t * group + i)

                @pl.when(jnp.logical_not(even) & (t == hold))
                def _():
                    @pl.loop(0, hold * group)
                    def _(h):
                        copy_of(h).start()

                @pl.when(even | (t >= hold))
                def _():
                    for i in range(group):
                        copy_of(t * group + i).start()

            for piece in range(2):
                arrived(other_side, piece).wait()

    def middle_device():
        @pl.when(has_below & has_above)
        def _():
            for side in (key_side, query_side):
                for piece in range(2):
                    arrived(side, piece).wait()
            enter_kernel()

            @pl.loop(0, groups)
            def _(t):
                for i in range(group):
                    h = t * group + i
                    from_keys(h)
                    from_queries(h)

    def within(first):
        causal = lax.broadcasted_iota(jnp.int32, (rows, rows), 0) >= lax.broadcasted_iota(jnp.int32, (rows, rows), 1)
        for i in range(group):
            h = first * group + i
            along = jnp.broadcast_to(cum[pl.ds(h, 1), :], (rows, rows))
            down_rows = along.T
            enter = jnp.exp(down_rows[:, :dim])
            leave = jnp.exp(down_rows[rows - 1:, :dim] - down_rows[:, :dim])
            decay_in[h], decay_out[h] = enter, leave
            q, k, v, g = q_ref[h], k_ref[h], v_ref[h], g_ref[h]
            q_dec[h] = (q.astype(jnp.float32) * enter).astype(jnp.bfloat16)
            k_dec[h] = (k.astype(jnp.float32) * leave).astype(jnp.bfloat16)
            weight = jnp.exp(jnp.where(causal, down_rows - along, -1e30))
            weighted[h] = (dot(q, k, (1, 1)) * weight).astype(jnp.bfloat16)
            weighted_grad[h] = (dot(g, v, (1, 1)) * weight).astype(jnp.bfloat16)

    def forward(h):
        @pl.when(has_below)
        def _():
            up_copy(h).wait_recv()

            @pl.when(has_above)
            def _():
                gain = gains[pl.ds(h, 1), :]
                up[h] = (gain * prefix[h].astype(jnp.float32) + state[h]).astype(jnp.bfloat16)
                up_copy(h).start()

    def backward(h):
        @pl.when(has_above)
        def _():
            down_copy(h).wait_recv()

            @pl.when(has_below)
            def _():
                gain = gains[pl.ds(h, 1), :]
                down[h] = (gain * suffix[h].astype(jnp.float32) + grad_state[h]).astype(jnp.bfloat16)
                down_copy(h).start()

    def finish_out(h):
        attn[h] = (dot(weighted[h], v_ref[h], (1, 0)) + dot(q_dec[h], prefix[h], (1, 0))).astype(jnp.bfloat16)

    def finish_queries(h):
        gq_ref[h] = (dot(weighted_grad[h], k_ref[h], (1, 0)) + dot(g_ref[h], prefix[h], (1, 1)) * decay_in[h]).astype(jnp.bfloat16)

    def send_out(h):
        @pl.when(sends)
        def _():
            for other in range(exp_count):
                attn_copy(h, other).start()

    def finish_backward(h):
        low = suffix[h]
        gk_ref[h] = (dot(weighted_grad[h], q_ref[h], (0, 0)) + dot(v_ref[h], low, (1, 1)) * decay_out[h]).astype(jnp.bfloat16)
        gv_ref[h] = (dot(weighted[h], g_ref[h], (0, 0)) + dot(k_dec[h], low, (1, 0))).astype(jnp.bfloat16)

    end_device(jnp.logical_not(has_below), key_side, from_keys, query_side, up_copy)
    end_device(has_below & jnp.logical_not(has_above), query_side, from_queries, key_side, down_copy)
    middle_device()

    @pl.loop(0, groups)
    def _(t):
        within(t)

    @pl.when(even & sends)
    def _():
        pl.semaphore_wait(ready, exp_count)

    @pl.loop(0, heads + max(UP_LAG, DOWN_LAG) * (seq_count - 1) // LAG_UNIT)
    def _(t):
        ahead = t - UP_LAG * seq // LAG_UNIT
        behind = t - DOWN_LAG * (seq_count - 1 - seq) // LAG_UNIT
        moves_up = (ahead >= 0) & (ahead < heads)
        moves_down = (behind >= 0) & (behind < heads)

        @pl.when(moves_up)
        def _():
            forward(ahead)

        @pl.when(moves_down)
        def _():
            backward(behind)

        @pl.when(moves_up)
        def _():
            finish_out(ahead)
            send_out(ahead)
            finish_queries(ahead)

        @pl.when(moves_down & jnp.logical_not(middle))
        def _():
            finish_backward(behind)

    @pl.when(middle)
    def _():
        @pl.loop(0, groups)
        def _(t):
            for i in range(group):
                finish_backward(t * group + i)

    @pl.when(has_above)
    def _():
        pltpu.make_async_copy(up, up, up_sem).wait()

    @pl.when(has_below)
    def _():
        pltpu.make_async_copy(down, down, down_sem).wait()

    @pl.when(sends)
    def _():
        pltpu.make_async_copy(attn, attn, attn_sem).wait()

    @pl.when(receives)
    def _():
        pltpu.make_async_copy(next_ref, next_ref, next_sem).wait()


def store(*refs):
    sem = refs[8]
    copies = [pltpu.make_async_copy(refs[i], refs[4 + i], sem.at[i]) for i in range(4)]
    for copy in copies:
        copy.start()
    for copy in copies:
        copy.wait()


def body(sizes, queries, keys, values, grad_out, log_decay):
    seq_count, pipe_count, exp_count = sizes
    _, heads, rows, dim = queries.shape
    group = math.gcd(GROUP, heads)
    low = jax.ShapeDtypeStruct((heads, rows, dim), jnp.bfloat16)
    vmem = pl.BlockSpec(memory_space=pltpu.VMEM)
    low_buf = pltpu.VMEM((heads, rows, dim), jnp.bfloat16)
    state_low = pltpu.VMEM((heads, dim, dim), jnp.bfloat16)
    state_wide = pltpu.VMEM((heads, dim, dim), jnp.float32)
    square_low = pltpu.VMEM((heads, rows, rows), jnp.bfloat16)
    wide = pltpu.VMEM((heads, rows, dim), jnp.float32)
    by_row = pltpu.VMEM((heads, rows), jnp.float32)
    dma = pltpu.SemaphoreType.DMA
    any_place = pl.BlockSpec(memory_space=pl.ANY)
    next_rows = (rows // exp_count, exp_count * heads * dim)
    outs = pl.pallas_call(
        functools.partial(kernel, sizes, group),
        out_shape=(pltpu.VMEM(next_rows, jnp.bfloat16), low_buf, low_buf, low_buf),
        in_specs=[pl.BlockSpec(memory_space=pltpu.HBM)] * 5,
        out_specs=(vmem,) * 4,
        scratch_shapes=[
            pltpu.VMEM((4, heads, rows, dim), jnp.bfloat16), by_row, by_row, by_row, by_row, pltpu.VMEM((heads, dim), jnp.float32),
            state_wide, state_wide, low_buf, low_buf, wide, wide, square_low, square_low,
            state_low, state_low, state_low, state_low, low_buf,
            dma((2, 2)), dma, dma((heads,)), dma((heads,)), dma, dma, dma, dma, pltpu.SemaphoreType.REGULAR,
        ],
        compiler_params=pltpu.CompilerParams(collective_id=0, has_side_effects=True, vmem_limit_bytes=VMEM_LIMIT),
    )(*(pltpu.with_memory_space_constraint(part[0], pltpu.HBM) for part in (queries, keys, values, grad_out, log_decay)))
    outs = pl.pallas_call(
        store,
        out_shape=(jax.ShapeDtypeStruct(next_rows, jnp.bfloat16), low, low, low),
        in_specs=[any_place] * 4,
        out_specs=(any_place,) * 4,
        scratch_shapes=[dma((4,))],
        compiler_params=pltpu.CompilerParams(vmem_limit_bytes=2**20),
    )(*outs)
    return tuple(out[None] for out in outs)


def solution(mesh):
    placed = P("pipe", "exp", "seq", None)
    sizes = tuple(mesh.shape[axis] for axis in ("seq", "pipe", "exp"))
    return jax.shard_map(
        functools.partial(body, sizes),
        mesh=mesh,
        in_specs=(placed, placed, placed, placed, P("pipe", "exp", "seq")),
        out_specs=(P("pipe", ("seq", "exp"), None), placed, placed, placed),
        check_vma=False,
    )
```

```python
import functools
import math

import jax
import jax.numpy as jnp
from jax import lax
from jax.experimental import pallas as pl
from jax.experimental.pallas import tpu as pltpu
from jax.sharding import PartitionSpec as P

MESH = pl.DeviceIdType.MESH
LAG_UNIT = 3
GROUP = 4
HOLD = 2
VMEM_LIMIT = 61 * 2**20


def dot(left, right, dims):
    return lax.dot_general(left, right, ((dims[:1], dims[1:]), ((), ())), preferred_element_type=jnp.float32)


def kernel(
    sizes, group, q_in, k_in, v_in, g_in, decay_in_ref, next_ref, gq_ref, gk_ref, gv_ref,
    loaded, decay_ref, cum, enter_rows, leave_rows, gains, state, grad_state, q_dec, k_dec, decay_in, decay_out,
    weighted, weighted_grad,
    prefix, suffix, up, down, attn,
    in_sem, decay_sem, prefix_sem, suffix_sem, up_sem, down_sem, attn_sem, next_sem, ready,
):
    seq_count, pipe_count, exp_count = sizes
    seq, pipe, exp = lax.axis_index("seq"), lax.axis_index("pipe"), lax.axis_index("exp")
    k_ref, v_ref, q_ref, g_ref = (loaded.at[i] for i in range(4))
    heads, rows, dim = loaded.shape[1:]
    groups = heads // group
    hold = min(HOLD, groups - 1)
    part_rows = rows // exp_count
    has_below, has_above = seq > 0, seq < seq_count - 1
    middle = has_below & has_above
    receives, sends = pipe > 0, pipe < pipe_count - 1
    even = pipe % 2 == 0
    final = pipe >= pipe_count - 2
    up_lag, down_lag = jnp.where(final, 12, 14), jnp.where(final, 15, 16)
    upper = 2 * seq >= seq_count

    decay_copy = pltpu.make_async_copy(decay_in_ref, decay_ref, decay_sem)
    decay_copy.start()

    barrier = pltpu.get_barrier_semaphore()

    def greet(condition, device):
        @pl.when(condition)
        def _():
            pl.semaphore_signal(barrier, inc=1, device_id=device, device_id_type=MESH)


    key_side, query_side = 0, 1

    def heads_of(piece):
        return pl.ds(1, heads - 1) if piece else pl.ds(0, 1)

    def arrived(side, piece):
        both = loaded.at[pl.ds(2 * side, 2), heads_of(piece)]
        return pltpu.make_async_copy(both, both, in_sem.at[side, piece])

    def load(side, piece):
        for i in range(2):
            src = ((k_in, v_in), (q_in, g_in))[side][i].at[heads_of(piece)]
            pltpu.make_async_copy(src, loaded.at[2 * side + i, heads_of(piece)], in_sem.at[side, piece]).start()

    @pl.when(upper)
    def _():
        load(query_side, 0)

    @pl.when(jnp.logical_not(upper))
    def _():
        load(key_side, 0)

    greet(has_below, {"seq": seq - 1})
    greet(has_above, {"seq": seq + 1})

    for other in range(exp_count):
        greet(even & receives, {"pipe": pipe - 1, "exp": other})
        greet(even & sends, {"pipe": pipe + 1, "exp": other})

    @pl.when(upper)
    def _():
        load(query_side, 1)
        load(key_side, 0)
        load(key_side, 1)

    @pl.when(jnp.logical_not(upper))
    def _():
        load(key_side, 1)
        load(query_side, 0)
        load(query_side, 1)

    def enter_kernel():
        beside = has_below.astype(jnp.int32) + has_above.astype(jnp.int32)
        relayed = receives.astype(jnp.int32) + sends.astype(jnp.int32)

        @pl.when(even)
        def _():
            pl.semaphore_wait(barrier, beside)

        @pl.when(jnp.logical_not(even))
        def _():
            pl.semaphore_wait(barrier, beside + exp_count * relayed)
            for other in range(exp_count):
                pl.semaphore_signal(ready, inc=1, device_id={"pipe": pipe - 1, "exp": other}, device_id_type=MESH)

    @pl.when(jnp.logical_not(has_below))
    def _():
        prefix[...] = jnp.zeros_like(prefix)

    @pl.when(jnp.logical_not(has_above))
    def _():
        suffix[...] = jnp.zeros_like(suffix)

    @pl.when(jnp.logical_not(receives))
    def _():
        next_ref[...] = jnp.zeros_like(next_ref)

    decay_copy.wait()
    rates, parts = decay_ref[...], []
    for _ in range(3):
        parts.append(rates.astype(jnp.bfloat16))
        rates = rates - parts[-1].astype(jnp.float32)
    upto = lax.broadcasted_iota(jnp.int32, (rows, rows), 0) <= lax.broadcasted_iota(jnp.int32, (rows, rows), 1)
    ones = jnp.where(upto, 1.0, 0.0).astype(jnp.bfloat16)
    total = dot(parts[2], ones, (1, 0)) + dot(parts[1], ones, (1, 0)) + dot(parts[0], ones, (1, 0))
    last = total[:, rows - 1:]
    cum[...] = total
    enter_rows[...] = jnp.exp(total)
    leave_rows[...] = jnp.exp(last - total)
    gains[...] = jnp.broadcast_to(jnp.exp(last), gains.shape)

    def up_copy(h):
        return pltpu.make_async_remote_copy(
            src_ref=up.at[h], dst_ref=prefix.at[h], send_sem=up_sem, recv_sem=prefix_sem.at[h],
            device_id={"seq": seq + 1}, device_id_type=MESH)

    def down_copy(h):
        return pltpu.make_async_remote_copy(
            src_ref=down.at[h], dst_ref=suffix.at[h], send_sem=down_sem, recv_sem=suffix_sem.at[h],
            device_id={"seq": seq - 1}, device_id_type=MESH)

    def attn_copy(head, other):
        place = pl.ds(pl.multiple_of((exp * heads + head) * dim, dim), dim)
        return pltpu.make_async_remote_copy(
            src_ref=attn.at[head, pl.ds(other * part_rows, part_rows)], dst_ref=next_ref.at[:, place],
            send_sem=attn_sem, recv_sem=next_sem,
            device_id={"pipe": pipe + 1, "exp": other}, device_id_type=MESH)

    def scaled(ref, decay_rows, h):
        return (ref[h].T.astype(jnp.float32) * decay_rows[pl.ds(h, 1), :]).astype(jnp.bfloat16)

    def from_keys(h):
        own = dot(scaled(k_ref, leave_rows, h), v_ref[h], (1, 0))
        state[h], up[h] = own, own.astype(jnp.bfloat16)

    def from_queries(h):
        own = dot(scaled(q_ref, enter_rows, h), g_ref[h], (1, 0))
        grad_state[h], down[h] = own, own.astype(jnp.bfloat16)

    def end_device(condition, side, one, other_side, copy_of):
        @pl.when(condition)
        def _():
            arrived(side, 0).wait()
            one(0)
            enter_kernel()

            @pl.when(even)
            def _():
                copy_of(0).start()

            arrived(side, 1).wait()
            for h in range(1, group):
                one(h)

            @pl.when(even)
            def _():
                for h in range(1, group):
                    copy_of(h).start()

            @pl.loop(1, groups)
            def _(t):
                for i in range(group):
                    one(t * group + i)

                @pl.when(jnp.logical_not(even) & (t == hold))
                def _():
                    @pl.loop(0, hold * group)
                    def _(h):
                        copy_of(h).start()

                @pl.when(even | (t >= hold))
                def _():
                    for i in range(group):
                        copy_of(t * group + i).start()

            for piece in range(2):
                arrived(other_side, piece).wait()

    def middle_device():
        @pl.when(has_below & has_above)
        def _():
            for side in (key_side, query_side):
                for piece in range(2):
                    arrived(side, piece).wait()
            enter_kernel()

            @pl.loop(0, groups)
            def _(t):
                for i in range(group):
                    h = t * group + i
                    from_keys(h)
                    from_queries(h)

    def within(first):
        causal = lax.broadcasted_iota(jnp.int32, (rows, rows), 0) >= lax.broadcasted_iota(jnp.int32, (rows, rows), 1)
        for i in range(group):
            h = first * group + i
            along = jnp.broadcast_to(cum[pl.ds(h, 1), :], (rows, rows))
            down_rows = along.T
            enter = jnp.exp(down_rows[:, :dim])
            leave = jnp.exp(down_rows[rows - 1:, :dim] - down_rows[:, :dim])
            decay_in[h], decay_out[h] = enter, leave
            q, k, v, g = q_ref[h], k_ref[h], v_ref[h], g_ref[h]
            q_dec[h] = (q.astype(jnp.float32) * enter).astype(jnp.bfloat16)
            k_dec[h] = (k.astype(jnp.float32) * leave).astype(jnp.bfloat16)
            weight = jnp.exp(jnp.where(causal, down_rows - along, -1e30))
            weighted[h] = (dot(q, k, (1, 1)) * weight).astype(jnp.bfloat16)
            weighted_grad[h] = (dot(g, v, (1, 1)) * weight).astype(jnp.bfloat16)

    def forward(h):
        @pl.when(has_below)
        def _():
            up_copy(h).wait_recv()

            @pl.when(has_above)
            def _():
                gain = gains[pl.ds(h, 1), :]
                up[h] = (gain * prefix[h].astype(jnp.float32) + state[h]).astype(jnp.bfloat16)
                up_copy(h).start()

    def backward(h):
        @pl.when(has_above)
        def _():
            down_copy(h).wait_recv()

            @pl.when(has_below)
            def _():
                gain = gains[pl.ds(h, 1), :]
                down[h] = (gain * suffix[h].astype(jnp.float32) + grad_state[h]).astype(jnp.bfloat16)
                down_copy(h).start()

    def finish_out(h):
        attn[h] = (dot(weighted[h], v_ref[h], (1, 0)) + dot(q_dec[h], prefix[h], (1, 0))).astype(jnp.bfloat16)

    def finish_queries(h):
        gq_ref[h] = (dot(weighted_grad[h], k_ref[h], (1, 0)) + dot(g_ref[h], prefix[h], (1, 1)) * decay_in[h]).astype(jnp.bfloat16)

    def send_out(h):
        @pl.when(sends)
        def _():
            for other in range(exp_count):
                attn_copy(h, other).start()

    def finish_backward(h):
        low = suffix[h]
        gk_ref[h] = (dot(weighted_grad[h], q_ref[h], (0, 0)) + dot(v_ref[h], low, (1, 1)) * decay_out[h]).astype(jnp.bfloat16)
        gv_ref[h] = (dot(weighted[h], g_ref[h], (0, 0)) + dot(k_dec[h], low, (1, 0))).astype(jnp.bfloat16)

    end_device(jnp.logical_not(has_below), key_side, from_keys, query_side, up_copy)
    end_device(has_below & jnp.logical_not(has_above), query_side, from_queries, key_side, down_copy)
    middle_device()

    @pl.loop(0, groups)
    def _(t):
        within(t)

    @pl.when(even & sends)
    def _():
        pl.semaphore_wait(ready, exp_count)

    @pl.loop(0, heads + jnp.maximum(up_lag, down_lag) * (seq_count - 1) // LAG_UNIT)
    def _(t):
        ahead = t - up_lag * seq // LAG_UNIT
        behind = t - down_lag * (seq_count - 1 - seq) // LAG_UNIT
        moves_up = (ahead >= 0) & (ahead < heads)
        moves_down = (behind >= 0) & (behind < heads)

        @pl.when(moves_up)
        def _():
            forward(ahead)

        @pl.when(moves_down)
        def _():
            backward(behind)

        @pl.when(moves_up)
        def _():
            finish_out(ahead)
            send_out(ahead)
            finish_queries(ahead)

        @pl.when(moves_down & jnp.logical_not(middle))
        def _():
            finish_backward(behind)

    @pl.when(middle)
    def _():
        @pl.loop(0, groups)
        def _(t):
            for i in range(group):
                finish_backward(t * group + i)

    @pl.when(has_above)
    def _():
        pltpu.make_async_copy(up, up, up_sem).wait()

    @pl.when(has_below)
    def _():
        pltpu.make_async_copy(down, down, down_sem).wait()

    @pl.when(sends)
    def _():
        pltpu.make_async_copy(attn, attn, attn_sem).wait()

    @pl.when(receives)
    def _():
        pltpu.make_async_copy(next_ref, next_ref, next_sem).wait()


def store(*refs):
    sem = refs[8]
    copies = [pltpu.make_async_copy(refs[i], refs[4 + i], sem.at[i]) for i in range(4)]
    for copy in copies:
        copy.start()
    for copy in copies:
        copy.wait()


def body(sizes, queries, keys, values, grad_out, log_decay):
    seq_count, pipe_count, exp_count = sizes
    _, heads, rows, dim = queries.shape
    group = math.gcd(GROUP, heads)
    low = jax.ShapeDtypeStruct((heads, rows, dim), jnp.bfloat16)
    vmem = pl.BlockSpec(memory_space=pltpu.VMEM)
    low_buf = pltpu.VMEM((heads, rows, dim), jnp.bfloat16)
    state_low = pltpu.VMEM((heads, dim, dim), jnp.bfloat16)
    state_wide = pltpu.VMEM((heads, dim, dim), jnp.float32)
    square_low = pltpu.VMEM((heads, rows, rows), jnp.bfloat16)
    wide = pltpu.VMEM((heads, rows, dim), jnp.float32)
    by_row = pltpu.VMEM((heads, rows), jnp.float32)
    dma = pltpu.SemaphoreType.DMA
    any_place = pl.BlockSpec(memory_space=pl.ANY)
    next_rows = (rows // exp_count, exp_count * heads * dim)
    outs = pl.pallas_call(
        functools.partial(kernel, sizes, group),
        out_shape=(pltpu.VMEM(next_rows, jnp.bfloat16), low_buf, low_buf, low_buf),
        in_specs=[pl.BlockSpec(memory_space=pltpu.HBM)] * 5,
        out_specs=(vmem,) * 4,
        scratch_shapes=[
            pltpu.VMEM((4, heads, rows, dim), jnp.bfloat16), by_row, by_row, by_row, by_row, pltpu.VMEM((heads, dim), jnp.float32),
            state_wide, state_wide, low_buf, low_buf, wide, wide, square_low, square_low,
            state_low, state_low, state_low, state_low, low_buf,
            dma((2, 2)), dma, dma((heads,)), dma((heads,)), dma, dma, dma, dma, pltpu.SemaphoreType.REGULAR,
        ],
        compiler_params=pltpu.CompilerParams(collective_id=0, has_side_effects=True, vmem_limit_bytes=VMEM_LIMIT),
    )(*(pltpu.with_memory_space_constraint(part[0], pltpu.HBM) for part in (queries, keys, values, grad_out, log_decay)))
    outs = pl.pallas_call(
        store,
        out_shape=(jax.ShapeDtypeStruct(next_rows, jnp.bfloat16), low, low, low),
        in_specs=[any_place] * 4,
        out_specs=(any_place,) * 4,
        scratch_shapes=[dma((4,))],
        compiler_params=pltpu.CompilerParams(vmem_limit_bytes=2**20),
    )(*outs)
    return tuple(out[None] for out in outs)


def solution(mesh):
    placed = P("pipe", "exp", "seq", None)
    sizes = tuple(mesh.shape[axis] for axis in ("seq", "pipe", "exp"))
    return jax.shard_map(
        functools.partial(body, sizes),
        mesh=mesh,
        in_specs=(placed, placed, placed, placed, P("pipe", "exp", "seq")),
        out_specs=(P("pipe", ("seq", "exp"), None), placed, placed, placed),
        check_vma=False,
    )
```

```python
import functools
import math

import jax
import jax.numpy as jnp
from jax import lax
from jax.experimental import pallas as pl
from jax.experimental.pallas import tpu as pltpu
from jax.sharding import PartitionSpec as P

MESH = pl.DeviceIdType.MESH
DOWN_LAG = 16
UP_LAG = 14
LAG_UNIT = 3
GROUP = 4
HOLD = 3
VMEM_LIMIT = 61 * 2**20


def dot(left, right, dims):
    return lax.dot_general(left, right, ((dims[:1], dims[1:]), ((), ())), preferred_element_type=jnp.float32)


def kernel(
    sizes, group, q_in, k_in, v_in, g_in, decay_in_ref, next_ref, gq_ref, gk_ref, gv_ref,
    loaded, decay_ref, cum, enter_rows, leave_rows, gains, state, grad_state, q_dec, k_dec, decay_in, decay_out,
    weighted, weighted_grad,
    prefix, suffix, up, down, attn,
    in_sem, decay_sem, prefix_sem, suffix_sem, out_sem, next_sem, ready,
):
    seq_count, pipe_count, exp_count = sizes
    seq, pipe, exp = lax.axis_index("seq"), lax.axis_index("pipe"), lax.axis_index("exp")
    k_ref, v_ref, q_ref, g_ref = (loaded.at[i] for i in range(4))
    heads, rows, dim = loaded.shape[1:]
    groups = heads // group
    hold = min(HOLD, groups - 1)
    part_rows = rows // exp_count
    has_below, has_above = seq > 0, seq < seq_count - 1
    middle = has_below & has_above
    receives, sends = pipe > 0, pipe < pipe_count - 1
    even = pipe % 2 == 0
    upper = 2 * seq >= seq_count

    decay_copy = pltpu.make_async_copy(decay_in_ref, decay_ref, decay_sem)
    decay_copy.start()

    barrier = pltpu.get_barrier_semaphore()

    def greet(condition, device):
        @pl.when(condition)
        def _():
            pl.semaphore_signal(barrier, inc=1, device_id=device, device_id_type=MESH)


    key_side, query_side = 0, 1

    def heads_of(piece):
        return pl.ds(1, heads - 1) if piece else pl.ds(0, 1)

    def arrived(side, piece):
        both = loaded.at[pl.ds(2 * side, 2), heads_of(piece)]
        return pltpu.make_async_copy(both, both, in_sem.at[side, piece])

    def load(side, piece):
        for i in range(2):
            src = ((k_in, v_in), (q_in, g_in))[side][i].at[heads_of(piece)]
            pltpu.make_async_copy(src, loaded.at[2 * side + i, heads_of(piece)], in_sem.at[side, piece]).start()

    @pl.when(upper)
    def _():
        load(query_side, 0)

    @pl.when(jnp.logical_not(upper))
    def _():
        load(key_side, 0)

    greet(has_below, {"seq": seq - 1})
    greet(has_above, {"seq": seq + 1})

    for other in range(exp_count):
        greet(even & receives, {"pipe": pipe - 1, "exp": other})
        greet(even & sends, {"pipe": pipe + 1, "exp": other})

    @pl.when(upper)
    def _():
        load(query_side, 1)
        load(key_side, 0)
        load(key_side, 1)

    @pl.when(jnp.logical_not(upper))
    def _():
        load(key_side, 1)
        load(query_side, 0)
        load(query_side, 1)

    def enter_kernel():
        beside = has_below.astype(jnp.int32) + has_above.astype(jnp.int32)
        relayed = receives.astype(jnp.int32) + sends.astype(jnp.int32)

        @pl.when(even)
        def _():
            pl.semaphore_wait(barrier, beside)

        @pl.when(jnp.logical_not(even))
        def _():
            pl.semaphore_wait(barrier, beside + exp_count * relayed)
            for other in range(exp_count):
                pl.semaphore_signal(ready, inc=1, device_id={"pipe": pipe - 1, "exp": other}, device_id_type=MESH)

    @pl.when(jnp.logical_not(has_below))
    def _():
        prefix[...] = jnp.zeros_like(prefix)

    @pl.when(jnp.logical_not(has_above))
    def _():
        suffix[...] = jnp.zeros_like(suffix)

    @pl.when(jnp.logical_not(receives))
    def _():
        next_ref[...] = jnp.zeros_like(next_ref)

    decay_copy.wait()
    rates, parts = decay_ref[...], []
    for _ in range(3):
        parts.append(rates.astype(jnp.bfloat16))
        rates = rates - parts[-1].astype(jnp.float32)
    upto = lax.broadcasted_iota(jnp.int32, (rows, rows), 0) <= lax.broadcasted_iota(jnp.int32, (rows, rows), 1)
    ones = jnp.where(upto, 1.0, 0.0).astype(jnp.bfloat16)
    total = dot(parts[2], ones, (1, 0)) + dot(parts[1], ones, (1, 0)) + dot(parts[0], ones, (1, 0))
    last = total[:, rows - 1:]
    cum[...] = total
    enter_rows[...] = jnp.exp(total)
    leave_rows[...] = jnp.exp(last - total)
    gains[...] = jnp.broadcast_to(jnp.exp(last), gains.shape)

    def up_copy(h):
        return pltpu.make_async_remote_copy(
            src_ref=up.at[h], dst_ref=prefix.at[h], send_sem=out_sem, recv_sem=prefix_sem.at[h],
            device_id={"seq": seq + 1}, device_id_type=MESH)

    def down_copy(h):
        return pltpu.make_async_remote_copy(
            src_ref=down.at[h], dst_ref=suffix.at[h], send_sem=out_sem, recv_sem=suffix_sem.at[h],
            device_id={"seq": seq - 1}, device_id_type=MESH)

    def attn_copy(head, other):
        place = pl.ds(pl.multiple_of((exp * heads + head) * dim, dim), dim)
        return pltpu.make_async_remote_copy(
            src_ref=attn.at[head, pl.ds(other * part_rows, part_rows)], dst_ref=next_ref.at[:, place],
            send_sem=out_sem, recv_sem=next_sem,
            device_id={"pipe": pipe + 1, "exp": other}, device_id_type=MESH)

    def scaled(ref, decay_rows, h):
        return (ref[h].T.astype(jnp.float32) * decay_rows[pl.ds(h, 1), :]).astype(jnp.bfloat16)

    def from_keys(h):
        own = dot(scaled(k_ref, leave_rows, h), v_ref[h], (1, 0))
        state[h], up[h] = own, own.astype(jnp.bfloat16)

    def from_queries(h):
        own = dot(scaled(q_ref, enter_rows, h), g_ref[h], (1, 0))
        grad_state[h], down[h] = own, own.astype(jnp.bfloat16)

    def end_device(condition, side, one, other_side, copy_of):
        @pl.when(condition)
        def _():
            arrived(side, 0).wait()
            one(0)
            enter_kernel()

            @pl.when(even)
            def _():
                copy_of(0).start()

            arrived(side, 1).wait()
            for h in range(1, group):
                one(h)

            @pl.when(even)
            def _():
                for h in range(1, group):
                    copy_of(h).start()

            @pl.loop(1, groups)
            def _(t):
                for i in range(group):
                    one(t * group + i)

                @pl.when(jnp.logical_not(even) & (t == hold))
                def _():
                    @pl.loop(0, hold * group)
                    def _(h):
                        copy_of(h).start()

                @pl.when(even | (t >= hold))
                def _():
                    for i in range(group):
                        copy_of(t * group + i).start()

            for piece in range(2):
                arrived(other_side, piece).wait()

    def middle_device():
        @pl.when(has_below & has_above)
        def _():
            for side in (key_side, query_side):
                for piece in range(2):
                    arrived(side, piece).wait()
            enter_kernel()

            @pl.loop(0, groups)
            def _(t):
                for i in range(group):
                    h = t * group + i
                    from_keys(h)
                    from_queries(h)

    def within(first):
        causal = lax.broadcasted_iota(jnp.int32, (rows, rows), 0) >= lax.broadcasted_iota(jnp.int32, (rows, rows), 1)
        for i in range(group):
            h = first * group + i
            along = jnp.broadcast_to(cum[pl.ds(h, 1), :], (rows, rows))
            down_rows = along.T
            enter = jnp.exp(down_rows[:, :dim])
            leave = jnp.exp(down_rows[rows - 1:, :dim] - down_rows[:, :dim])
            decay_in[h], decay_out[h] = enter, leave
            q, k, v, g = q_ref[h], k_ref[h], v_ref[h], g_ref[h]
            q_dec[h] = (q.astype(jnp.float32) * enter).astype(jnp.bfloat16)
            k_dec[h] = (k.astype(jnp.float32) * leave).astype(jnp.bfloat16)
            weight = jnp.exp(jnp.where(causal, down_rows - along, -1e30))
            weighted[h] = (dot(q, k, (1, 1)) * weight).astype(jnp.bfloat16)
            weighted_grad[h] = (dot(g, v, (1, 1)) * weight).astype(jnp.bfloat16)

    def forward(h):
        @pl.when(has_below)
        def _():
            up_copy(h).wait_recv()

            @pl.when(has_above)
            def _():
                gain = gains[pl.ds(h, 1), :]
                up[h] = (gain * prefix[h].astype(jnp.float32) + state[h]).astype(jnp.bfloat16)
                up_copy(h).start()

    def backward(h):
        @pl.when(has_above)
        def _():
            down_copy(h).wait_recv()

            @pl.when(has_below)
            def _():
                gain = gains[pl.ds(h, 1), :]
                down[h] = (gain * suffix[h].astype(jnp.float32) + grad_state[h]).astype(jnp.bfloat16)
                down_copy(h).start()

    def finish_out(h):
        attn[h] = (dot(weighted[h], v_ref[h], (1, 0)) + dot(q_dec[h], prefix[h], (1, 0))).astype(jnp.bfloat16)

    def finish_queries(h):
        gq_ref[h] = (dot(weighted_grad[h], k_ref[h], (1, 0)) + dot(g_ref[h], prefix[h], (1, 1)) * decay_in[h]).astype(jnp.bfloat16)

    def send_out(h):
        @pl.when(sends)
        def _():
            for other in range(exp_count):
                attn_copy(h, other).start()

    def finish_backward(h):
        low = suffix[h]
        gk_ref[h] = (dot(weighted_grad[h], q_ref[h], (0, 0)) + dot(v_ref[h], low, (1, 1)) * decay_out[h]).astype(jnp.bfloat16)
        gv_ref[h] = (dot(weighted[h], g_ref[h], (0, 0)) + dot(k_dec[h], low, (1, 0))).astype(jnp.bfloat16)

    end_device(jnp.logical_not(has_below), key_side, from_keys, query_side, up_copy)
    end_device(has_below & jnp.logical_not(has_above), query_side, from_queries, key_side, down_copy)
    middle_device()

    @pl.loop(0, groups)
    def _(t):
        within(t)

    @pl.when(even & sends)
    def _():
        pl.semaphore_wait(ready, exp_count)

    @pl.loop(0, heads + max(UP_LAG, DOWN_LAG) * (seq_count - 1) // LAG_UNIT)
    def _(t):
        ahead = t - UP_LAG * seq // LAG_UNIT
        behind = t - DOWN_LAG * (seq_count - 1 - seq) // LAG_UNIT
        moves_up = (ahead >= 0) & (ahead < heads)
        moves_down = (behind >= 0) & (behind < heads)

        @pl.when(moves_up)
        def _():
            forward(ahead)

        @pl.when(moves_down)
        def _():
            backward(behind)

        @pl.when(moves_up)
        def _():
            finish_out(ahead)
            send_out(ahead)
            finish_queries(ahead)

        @pl.when(moves_down & jnp.logical_not(middle))
        def _():
            finish_backward(behind)

    @pl.when(middle)
    def _():
        @pl.loop(0, groups)
        def _(t):
            for i in range(group):
                finish_backward(t * group + i)

    @pl.when(has_above)
    def _():
        pltpu.make_async_copy(up, up, out_sem).wait()

    @pl.when(has_below)
    def _():
        pltpu.make_async_copy(down, down, out_sem).wait()

    @pl.when(sends)
    def _():
        pltpu.make_async_copy(attn, attn, out_sem).wait()

    @pl.when(receives)
    def _():
        pltpu.make_async_copy(next_ref, next_ref, next_sem).wait()


def store(*refs):
    sem = refs[8]
    copies = [pltpu.make_async_copy(refs[i], refs[4 + i], sem.at[i]) for i in range(4)]
    for copy in copies:
        copy.start()
    for copy in copies:
        copy.wait()


def body(sizes, queries, keys, values, grad_out, log_decay):
    seq_count, pipe_count, exp_count = sizes
    _, heads, rows, dim = queries.shape
    group = math.gcd(GROUP, heads)
    low = jax.ShapeDtypeStruct((heads, rows, dim), jnp.bfloat16)
    vmem = pl.BlockSpec(memory_space=pltpu.VMEM)
    low_buf = pltpu.VMEM((heads, rows, dim), jnp.bfloat16)
    state_low = pltpu.VMEM((heads, dim, dim), jnp.bfloat16)
    state_wide = pltpu.VMEM((heads, dim, dim), jnp.float32)
    square_low = pltpu.VMEM((heads, rows, rows), jnp.bfloat16)
    wide = pltpu.VMEM((heads, rows, dim), jnp.float32)
    by_row = pltpu.VMEM((heads, rows), jnp.float32)
    dma = pltpu.SemaphoreType.DMA
    any_place = pl.BlockSpec(memory_space=pl.ANY)
    next_rows = (rows // exp_count, exp_count * heads * dim)
    outs = pl.pallas_call(
        functools.partial(kernel, sizes, group),
        out_shape=(pltpu.VMEM(next_rows, jnp.bfloat16), low_buf, low_buf, low_buf),
        in_specs=[pl.BlockSpec(memory_space=pltpu.HBM)] * 5,
        out_specs=(vmem,) * 4,
        scratch_shapes=[
            pltpu.VMEM((4, heads, rows, dim), jnp.bfloat16), by_row, by_row, by_row, by_row, pltpu.VMEM((heads, dim), jnp.float32),
            state_wide, state_wide, low_buf, low_buf, wide, wide, square_low, square_low,
            state_low, state_low, state_low, state_low, low_buf,
            dma((2, 2)), dma, dma((heads,)), dma((heads,)), dma, dma, pltpu.SemaphoreType.REGULAR,
        ],
        compiler_params=pltpu.CompilerParams(collective_id=0, has_side_effects=True, vmem_limit_bytes=VMEM_LIMIT),
    )(*(pltpu.with_memory_space_constraint(part[0], pltpu.HBM) for part in (queries, keys, values, grad_out, log_decay)))
    outs = pl.pallas_call(
        store,
        out_shape=(jax.ShapeDtypeStruct(next_rows, jnp.bfloat16), low, low, low),
        in_specs=[any_place] * 4,
        out_specs=(any_place,) * 4,
        scratch_shapes=[dma((4,))],
        compiler_params=pltpu.CompilerParams(vmem_limit_bytes=2**20),
    )(*outs)
    return tuple(out[None] for out in outs)


def solution(mesh):
    placed = P("pipe", "exp", "seq", None)
    sizes = tuple(mesh.shape[axis] for axis in ("seq", "pipe", "exp"))
    return jax.shard_map(
        functools.partial(body, sizes),
        mesh=mesh,
        in_specs=(placed, placed, placed, placed, P("pipe", "exp", "seq")),
        out_specs=(P("pipe", ("seq", "exp"), None), placed, placed, placed),
        check_vma=False,
    )
```

```python
import functools
import math

import jax
import jax.numpy as jnp
from jax import lax
from jax.experimental import pallas as pl
from jax.experimental.pallas import tpu as pltpu
from jax.sharding import PartitionSpec as P

MESH = pl.DeviceIdType.MESH
LAG_UNIT = 3
GROUP = 4
HOLD = 3
VMEM_LIMIT = 61 * 2**20


def dot(left, right, dims):
    return lax.dot_general(left, right, ((dims[:1], dims[1:]), ((), ())), preferred_element_type=jnp.float32)


def kernel(
    sizes, group, q_in, k_in, v_in, g_in, decay_in_ref, next_ref, gq_ref, gk_ref, gv_ref,
    loaded, decay_ref, cum, enter_rows, leave_rows, gains, state, grad_state, q_dec, k_dec, decay_in, decay_out,
    weighted, weighted_grad,
    prefix, suffix, up, down, attn,
    in_sem, decay_sem, prefix_sem, suffix_sem, up_sem, down_sem, attn_sem, next_sem, ready,
):
    seq_count, pipe_count, exp_count = sizes
    seq, pipe, exp = lax.axis_index("seq"), lax.axis_index("pipe"), lax.axis_index("exp")
    k_ref, v_ref, q_ref, g_ref = (loaded.at[i] for i in range(4))
    heads, rows, dim = loaded.shape[1:]
    groups = heads // group
    hold = min(HOLD, groups - 1)
    part_rows = rows // exp_count
    has_below, has_above = seq > 0, seq < seq_count - 1
    middle = has_below & has_above
    receives, sends = pipe > 0, pipe < pipe_count - 1
    even = pipe % 2 == 0
    final = pipe >= pipe_count - 2
    up_lag, down_lag = jnp.where(final, 12, 14), jnp.where(final, 15, 16)
    upper = 2 * seq >= seq_count

    decay_copy = pltpu.make_async_copy(decay_in_ref, decay_ref, decay_sem)
    decay_copy.start()

    barrier = pltpu.get_barrier_semaphore()

    def greet(condition, device):
        @pl.when(condition)
        def _():
            pl.semaphore_signal(barrier, inc=1, device_id=device, device_id_type=MESH)


    key_side, query_side = 0, 1

    def heads_of(piece):
        return pl.ds(1, heads - 1) if piece else pl.ds(0, 1)

    def arrived(side, piece):
        both = loaded.at[pl.ds(2 * side, 2), heads_of(piece)]
        return pltpu.make_async_copy(both, both, in_sem.at[side, piece])

    def load(side, piece):
        for i in range(2):
            src = ((k_in, v_in), (q_in, g_in))[side][i].at[heads_of(piece)]
            pltpu.make_async_copy(src, loaded.at[2 * side + i, heads_of(piece)], in_sem.at[side, piece]).start()

    @pl.when(upper)
    def _():
        load(query_side, 0)

    @pl.when(jnp.logical_not(upper))
    def _():
        load(key_side, 0)

    greet(has_below, {"seq": seq - 1})
    greet(has_above, {"seq": seq + 1})

    for other in range(exp_count):
        greet(even & receives, {"pipe": pipe - 1, "exp": other})
        greet(even & sends, {"pipe": pipe + 1, "exp": other})

    @pl.when(upper)
    def _():
        load(query_side, 1)
        load(key_side, 0)
        load(key_side, 1)

    @pl.when(jnp.logical_not(upper))
    def _():
        load(key_side, 1)
        load(query_side, 0)
        load(query_side, 1)

    def enter_kernel():
        beside = has_below.astype(jnp.int32) + has_above.astype(jnp.int32)
        relayed = receives.astype(jnp.int32) + sends.astype(jnp.int32)

        @pl.when(even)
        def _():
            pl.semaphore_wait(barrier, beside)

        @pl.when(jnp.logical_not(even))
        def _():
            pl.semaphore_wait(barrier, beside + exp_count * relayed)
            for other in range(exp_count):
                pl.semaphore_signal(ready, inc=1, device_id={"pipe": pipe - 1, "exp": other}, device_id_type=MESH)

    @pl.when(jnp.logical_not(has_below))
    def _():
        prefix[...] = jnp.zeros_like(prefix)

    @pl.when(jnp.logical_not(has_above))
    def _():
        suffix[...] = jnp.zeros_like(suffix)

    @pl.when(jnp.logical_not(receives))
    def _():
        next_ref[...] = jnp.zeros_like(next_ref)

    decay_copy.wait()
    rates, parts = decay_ref[...], []
    for _ in range(3):
        parts.append(rates.astype(jnp.bfloat16))
        rates = rates - parts[-1].astype(jnp.float32)
    upto = lax.broadcasted_iota(jnp.int32, (rows, rows), 0) <= lax.broadcasted_iota(jnp.int32, (rows, rows), 1)
    ones = jnp.where(upto, 1.0, 0.0).astype(jnp.bfloat16)
    total = dot(parts[2], ones, (1, 0)) + dot(parts[1], ones, (1, 0)) + dot(parts[0], ones, (1, 0))
    last = total[:, rows - 1:]
    cum[...] = total
    enter_rows[...] = jnp.exp(total)
    leave_rows[...] = jnp.exp(last - total)
    gains[...] = jnp.broadcast_to(jnp.exp(last), gains.shape)

    def up_copy(h):
        return pltpu.make_async_remote_copy(
            src_ref=up.at[h], dst_ref=prefix.at[h], send_sem=up_sem, recv_sem=prefix_sem.at[h],
            device_id={"seq": seq + 1}, device_id_type=MESH)

    def down_copy(h):
        return pltpu.make_async_remote_copy(
            src_ref=down.at[h], dst_ref=suffix.at[h], send_sem=down_sem, recv_sem=suffix_sem.at[h],
            device_id={"seq": seq - 1}, device_id_type=MESH)

    def attn_copy(head, other):
        place = pl.ds(pl.multiple_of((exp * heads + head) * dim, dim), dim)
        return pltpu.make_async_remote_copy(
            src_ref=attn.at[head, pl.ds(other * part_rows, part_rows)], dst_ref=next_ref.at[:, place],
            send_sem=attn_sem, recv_sem=next_sem,
            device_id={"pipe": pipe + 1, "exp": other}, device_id_type=MESH)

    def scaled(ref, decay_rows, h):
        return (ref[h].T.astype(jnp.float32) * decay_rows[pl.ds(h, 1), :]).astype(jnp.bfloat16)

    def from_keys(h):
        own = dot(scaled(k_ref, leave_rows, h), v_ref[h], (1, 0))
        state[h], up[h] = own, own.astype(jnp.bfloat16)

    def from_queries(h):
        own = dot(scaled(q_ref, enter_rows, h), g_ref[h], (1, 0))
        grad_state[h], down[h] = own, own.astype(jnp.bfloat16)

    def end_device(condition, side, one, other_side, copy_of):
        @pl.when(condition)
        def _():
            arrived(side, 0).wait()
            one(0)
            enter_kernel()

            @pl.when(even)
            def _():
                copy_of(0).start()

            arrived(side, 1).wait()
            for h in range(1, group):
                one(h)

            @pl.when(even)
            def _():
                for h in range(1, group):
                    copy_of(h).start()

            @pl.loop(1, groups)
            def _(t):
                for i in range(group):
                    one(t * group + i)

                @pl.when(jnp.logical_not(even) & (t == hold))
                def _():
                    @pl.loop(0, hold * group)
                    def _(h):
                        copy_of(h).start()

                @pl.when(even | (t >= hold))
                def _():
                    for i in range(group):
                        copy_of(t * group + i).start()

            for piece in range(2):
                arrived(other_side, piece).wait()

    def middle_device():
        @pl.when(has_below & has_above)
        def _():
            for side in (key_side, query_side):
                for piece in range(2):
                    arrived(side, piece).wait()
            enter_kernel()

            @pl.loop(0, groups)
            def _(t):
                for i in range(group):
                    h = t * group + i
                    from_keys(h)
                    from_queries(h)

    def within(first):
        causal = lax.broadcasted_iota(jnp.int32, (rows, rows), 0) >= lax.broadcasted_iota(jnp.int32, (rows, rows), 1)
        for i in range(group):
            h = first * group + i
            along = jnp.broadcast_to(cum[pl.ds(h, 1), :], (rows, rows))
            down_rows = along.T
            enter = jnp.exp(down_rows[:, :dim])
            leave = jnp.exp(down_rows[rows - 1:, :dim] - down_rows[:, :dim])
            decay_in[h], decay_out[h] = enter, leave
            q, k, v, g = q_ref[h], k_ref[h], v_ref[h], g_ref[h]
            q_dec[h] = (q.astype(jnp.float32) * enter).astype(jnp.bfloat16)
            k_dec[h] = (k.astype(jnp.float32) * leave).astype(jnp.bfloat16)
            weight = jnp.exp(jnp.where(causal, down_rows - along, -1e30))
            weighted[h] = (dot(q, k, (1, 1)) * weight).astype(jnp.bfloat16)
            weighted_grad[h] = (dot(g, v, (1, 1)) * weight).astype(jnp.bfloat16)

    def forward(h):
        @pl.when(has_below)
        def _():
            up_copy(h).wait_recv()

            @pl.when(has_above)
            def _():
                gain = gains[pl.ds(h, 1), :]
                up[h] = (gain * prefix[h].astype(jnp.float32) + state[h]).astype(jnp.bfloat16)
                up_copy(h).start()

    def backward(h):
        @pl.when(has_above)
        def _():
            down_copy(h).wait_recv()

            @pl.when(has_below)
            def _():
                gain = gains[pl.ds(h, 1), :]
                down[h] = (gain * suffix[h].astype(jnp.float32) + grad_state[h]).astype(jnp.bfloat16)
                down_copy(h).start()

    def finish_out(h):
        attn[h] = (dot(weighted[h], v_ref[h], (1, 0)) + dot(q_dec[h], prefix[h], (1, 0))).astype(jnp.bfloat16)

    def finish_queries(h):
        gq_ref[h] = (dot(weighted_grad[h], k_ref[h], (1, 0)) + dot(g_ref[h], prefix[h], (1, 1)) * decay_in[h]).astype(jnp.bfloat16)

    def send_out(h):
        @pl.when(sends)
        def _():
            for other in range(exp_count):
                attn_copy(h, other).start()

    def finish_backward(h):
        low = suffix[h]
        gk_ref[h] = (dot(weighted_grad[h], q_ref[h], (0, 0)) + dot(v_ref[h], low, (1, 1)) * decay_out[h]).astype(jnp.bfloat16)
        gv_ref[h] = (dot(weighted[h], g_ref[h], (0, 0)) + dot(k_dec[h], low, (1, 0))).astype(jnp.bfloat16)

    end_device(jnp.logical_not(has_below), key_side, from_keys, query_side, up_copy)
    end_device(has_below & jnp.logical_not(has_above), query_side, from_queries, key_side, down_copy)
    middle_device()

    @pl.loop(0, groups)
    def _(t):
        within(t)

    @pl.when(even & sends)
    def _():
        pl.semaphore_wait(ready, exp_count)

    @pl.loop(0, heads + jnp.maximum(up_lag, down_lag) * (seq_count - 1) // LAG_UNIT)
    def _(t):
        ahead = t - up_lag * seq // LAG_UNIT
        behind = t - down_lag * (seq_count - 1 - seq) // LAG_UNIT
        moves_up = (ahead >= 0) & (ahead < heads)
        moves_down = (behind >= 0) & (behind < heads)

        @pl.when(moves_up)
        def _():
            forward(ahead)

        @pl.when(moves_down)
        def _():
            backward(behind)

        @pl.when(moves_up)
        def _():
            finish_out(ahead)
            send_out(ahead)
            finish_queries(ahead)

        @pl.when(moves_down & jnp.logical_not(middle))
        def _():
            finish_backward(behind)

    @pl.when(middle)
    def _():
        @pl.loop(0, groups)
        def _(t):
            for i in range(group):
                finish_backward(t * group + i)

    @pl.when(has_above)
    def _():
        pltpu.make_async_copy(up, up, up_sem).wait()

    @pl.when(has_below)
    def _():
        pltpu.make_async_copy(down, down, down_sem).wait()

    @pl.when(sends)
    def _():
        pltpu.make_async_copy(attn, attn, attn_sem).wait()

    @pl.when(receives)
    def _():
        pltpu.make_async_copy(next_ref, next_ref, next_sem).wait()


def store(*refs):
    sem = refs[8]
    copies = [pltpu.make_async_copy(refs[i], refs[4 + i], sem.at[i]) for i in range(4)]
    for copy in copies:
        copy.start()
    for copy in copies:
        copy.wait()


def body(sizes, queries, keys, values, grad_out, log_decay):
    seq_count, pipe_count, exp_count = sizes
    _, heads, rows, dim = queries.shape
    group = math.gcd(GROUP, heads)
    low = jax.ShapeDtypeStruct((heads, rows, dim), jnp.bfloat16)
    vmem = pl.BlockSpec(memory_space=pltpu.VMEM)
    low_buf = pltpu.VMEM((heads, rows, dim), jnp.bfloat16)
    state_low = pltpu.VMEM((heads, dim, dim), jnp.bfloat16)
    state_wide = pltpu.VMEM((heads, dim, dim), jnp.float32)
    square_low = pltpu.VMEM((heads, rows, rows), jnp.bfloat16)
    wide = pltpu.VMEM((heads, rows, dim), jnp.float32)
    by_row = pltpu.VMEM((heads, rows), jnp.float32)
    dma = pltpu.SemaphoreType.DMA
    any_place = pl.BlockSpec(memory_space=pl.ANY)
    next_rows = (rows // exp_count, exp_count * heads * dim)
    outs = pl.pallas_call(
        functools.partial(kernel, sizes, group),
        out_shape=(pltpu.VMEM(next_rows, jnp.bfloat16), low_buf, low_buf, low_buf),
        in_specs=[pl.BlockSpec(memory_space=pltpu.HBM)] * 5,
        out_specs=(vmem,) * 4,
        scratch_shapes=[
            pltpu.VMEM((4, heads, rows, dim), jnp.bfloat16), by_row, by_row, by_row, by_row, pltpu.VMEM((heads, dim), jnp.float32),
            state_wide, state_wide, low_buf, low_buf, wide, wide, square_low, square_low,
            state_low, state_low, state_low, state_low, low_buf,
            dma((2, 2)), dma, dma((heads,)), dma((heads,)), dma, dma, dma, dma, pltpu.SemaphoreType.REGULAR,
        ],
        compiler_params=pltpu.CompilerParams(collective_id=0, has_side_effects=True, vmem_limit_bytes=VMEM_LIMIT),
    )(*(pltpu.with_memory_space_constraint(part[0], pltpu.HBM) for part in (queries, keys, values, grad_out, log_decay)))
    outs = pl.pallas_call(
        store,
        out_shape=(jax.ShapeDtypeStruct(next_rows, jnp.bfloat16), low, low, low),
        in_specs=[any_place] * 4,
        out_specs=(any_place,) * 4,
        scratch_shapes=[dma((4,))],
        compiler_params=pltpu.CompilerParams(vmem_limit_bytes=2**20),
    )(*outs)
    return tuple(out[None] for out in outs)


def solution(mesh):
    placed = P("pipe", "exp", "seq", None)
    sizes = tuple(mesh.shape[axis] for axis in ("seq", "pipe", "exp"))
    return jax.shard_map(
        functools.partial(body, sizes),
        mesh=mesh,
        in_specs=(placed, placed, placed, placed, P("pipe", "exp", "seq")),
        out_specs=(P("pipe", ("seq", "exp"), None), placed, placed, placed),
        check_vma=False,
    )
```
